256 devices in a mesh: seq: 32 (over y, z), ch: 8 (over x, core).
Axes of the slice: x: 4, y: 4, z: 8, core: 2. Of those that a mesh axis runs over, the one named last changes fastest.
Arguments:
- signal: bfloat16 [4096, 8192], P('seq', 'ch'), may hold values from -6 to 6
- gate_values: bfloat16 [4096, 8192], P('seq', 'ch'), may hold values from -6 to 6
- filter_taps: bfloat16 [4096, 8192], P('seq', 'ch'), may hold values from -0.09375 to 0.09375
- skip_gain: float32 [8192], P(('ch', 'seq')), may hold values from -1 to 1
- w_out: bfloat16 [8192, 8192], P('ch', 'seq'), may hold values from -0.0625 to 0.0625
- cotangent: bfloat16 [4096, 8192], P('seq', 'ch'), may hold values from -6 to 6
Outputs:
- grad_input: bfloat16 [4096, 8192], P('seq', 'ch')
- grad_gate: bfloat16 [4096, 8192], P('seq', 'ch')
- grad_filter: bfloat16 [4096, 8192], P('seq', 'ch')
- grad_skip: float32 [8192], P(('ch', 'seq'))
- grad_weight: float32 [8192, 8192], P('ch', 'seq')
The draws below stay inside these ranges and needn't reach their ends.
All inputs are finite; a program needn't handle non-finite values.
Results may differ from the reference program's by a relative error of at most 0.005.
Values may be sent and summed in bfloat16 or wider, within the bound.
No kernel may reach another device: no remote copies, remote signals or barrier semaphores. Data moves between devices by JAX's collectives and lax.ppermute only.
A program may use at most 128 MiB of HBM per device.

```python
import math
import jax
import jax.numpy as jnp
from jax import lax

D = 8192
SEQ_LEN = 4096


def raised(array, stream_key, source, target, shards_of, factor):
    def block_of(dim):
        return (jnp.arange(array.shape[dim]) // (array.shape[dim] // shards_of)).reshape((-1,) + (1,) * (array.ndim - 1 - dim))

    near = jax.random.permutation(stream_key, shards_of)[block_of(target)]
    far = (block_of(target) + shards_of // 2) % shards_of
    return jnp.where((block_of(source) == near) | (block_of(source) == far), factor * array, array)


def levels(rng, dims, cuts, least, largest):
    def one(position, shards_of):
        heights = jax.random.uniform(jax.random.fold_in(jax.random.fold_in(rng, 6), position), (shards_of,), jnp.float32, least / len(cuts), largest / len(cuts))
        return jnp.repeat(jnp.exp(heights), dims[position] // shards_of).reshape((-1,) + (1,) * (len(dims) - position - 1))

    level = one(*cuts[0])
    for cut in cuts[1:]:
        level = level * one(*cut)
    return level


def bell_draw(key, shape, spread, most, cuts=(), kind=jnp.bfloat16):
    level = levels(key, shape, cuts, -0.22, 0.18) if cuts else 1.0
    array = jax.random.normal(key, shape, jnp.float32) * spread * level
    return jnp.minimum(jnp.maximum(array, -most), most).astype(kind)


def bell_draw_with(stream_key, shape, scale, limit, shards, heavy, dtype=jnp.bfloat16):
    drawn = scale * jax.random.normal(stream_key, shape, jnp.float32)
    if shards:
        drawn = drawn * levels(stream_key, shape, shards, -0.22, 0.18)
    return jnp.clip(raised(drawn, jax.random.fold_in(stream_key, 3), *heavy), -limit, limit).astype(dtype)


def setup_inputs(seed: int = 0) -> dict:
    seeds = jax.random.split(jax.random.key(seed), 7)
    return {
        "signal": bell_draw(seeds[0], (SEQ_LEN, D), 1.0, 6.0, ((0, 32), (1, 8))),
        "gate_values": bell_draw(seeds[1], (SEQ_LEN, D), 1.0, 6.0, ((0, 32), (1, 8))),
        "filter_taps": bell_draw(seeds[2], (SEQ_LEN, D), SEQ_LEN ** -0.5, 0.09375, ((0, 32), (1, 8))),
        "skip_gain": jnp.clip(jax.random.uniform(seeds[3], (D,), jnp.float32, -1.0, 1.0) * levels(seeds[3], (D,), ((0, 256),), -0.4, 0.0), -1.0, 1.0),
        "w_out": bell_draw(seeds[4], (D, D), D ** -0.5, 0.0625, ((0, 8), (1, 32))),
        "cotangent": bell_draw_with(seeds[5], (SEQ_LEN, D), 1.0, 6.0, ((0, 32), (1, 8)), (0, 1, 32, 2.75)),
    }


block_width = 256

def reference(signal, gate_values, filter_taps, skip_gain, w_out, cotangent):
    length = SEQ_LEN
    padded = 2 * length
    inv_root = 1.0 / math.sqrt(length)
    groups = D // block_width

    def by_blocks(matrix):
        return matrix.astype(jnp.float32).T.reshape(groups, block_width, length)

    def unblock(blocks):
        return blocks.reshape(D, length).T

    def forward_conv(pair):
        sig_block, tap_block = pair
        product = jnp.fft.rfft(sig_block, n=padded, axis=1) * jnp.fft.rfft(tap_block, n=padded, axis=1)
        return jnp.fft.irfft(product, n=padded, axis=1)[:, :length]

    def backward_conv(triple):
        grad_block, sig_block, tap_block = triple
        spec_grad = jnp.fft.rfft(grad_block, n=padded, axis=1)
        back_in = jnp.fft.irfft(spec_grad * jnp.conj(jnp.fft.rfft(tap_block, n=padded, axis=1)), n=padded, axis=1)[:, :length]
        back_tap = jnp.fft.irfft(spec_grad * jnp.conj(jnp.fft.rfft(sig_block, n=padded, axis=1)), n=padded, axis=1)[:, :length]
        return (back_in, back_tap)
    sig_blocks = by_blocks(signal)
    tap_blocks = by_blocks(filter_taps)
    conv_out = unblock(lax.map(forward_conv, (sig_blocks, tap_blocks)))
    signal32 = signal.astype(jnp.float32)
    mixed = (conv_out + skip_gain[None, :] * signal32).astype(jnp.bfloat16)
    gate32 = gate_values.astype(jnp.float32)
    mixed32 = mixed.astype(jnp.float32)
    gated = (gate32 * mixed32).astype(jnp.bfloat16)
    grad_gated = jnp.dot(cotangent, w_out.T, preferred_element_type=jnp.float32)
    grad_gate = (grad_gated * mixed32).astype(jnp.bfloat16)
    grad_mixed = (grad_gated * gate32).astype(jnp.bfloat16)
    grad_mixed32 = grad_mixed.astype(jnp.float32)
    back_in, back_tap = lax.map(backward_conv, (by_blocks(grad_mixed), sig_blocks, tap_blocks))
    grad_input = (unblock(back_in) + skip_gain[None, :] * grad_mixed32).astype(jnp.bfloat16)
    grad_filter = (unblock(back_tap) * inv_root).astype(jnp.bfloat16)
    grad_skip = lax.optimization_barrier(jnp.sum(grad_mixed32 * signal32, axis=0)) * inv_root
    grad_weight = jnp.dot(gated.T, cotangent, preferred_element_type=jnp.float32) * inv_root
    return (grad_input, grad_gate, grad_filter, grad_skip, grad_weight)
```

```python
import functools
import math

import jax
import jax.numpy as jnp
import numpy as np
from jax import lax
from jax.experimental import pallas as pl
from jax.experimental.pallas import tpu as pltpu
from jax.sharding import Mesh
from jax.sharding import PartitionSpec as P

NY, NZ, NX, NH = 4, 8, 4, 2
NS = NY * NZ
TOK = 128
CL = 32
CC = 16
FREQ = 2 * NS * TOK
ROOT = 1.0 / math.sqrt(NS * TOK)
bf16, f32 = jnp.bfloat16, jnp.float32


def halves(matrix):
    high = matrix.astype(jnp.bfloat16)
    low = (matrix - high.astype(np.float64)).astype(jnp.bfloat16)
    return high, low


def tables():
    k = np.arange(NS)[:, None] + 0.5
    n = np.arange(NS)[None, :]
    m = np.arange(TOK)[None, :]
    outer = 2.0 * np.pi * k * n / (2 * NS)
    a = np.concatenate([np.cos(outer), -np.sin(outer)], axis=0)
    a_inv = np.concatenate([np.cos(outer).T, -np.sin(outer).T], axis=1) * (2.0 / FREQ)
    turn = 2.0 * np.pi * k * m / FREQ
    inner = 2.0 * np.pi * (np.arange(TOK)[:, None] * m % TOK) / TOK
    c, s = np.cos(inner), np.sin(inner)
    b = np.block([[c, -s], [s, c]])
    b_inv = np.block([[c, s], [-s, c]])
    a_hi, a_lo = halves(a)
    i_hi, i_lo = halves(a_inv)
    b_hi, b_lo = halves(b)
    v_hi, v_lo = halves(b_inv)
    return (
        np.concatenate([a_hi, a_lo], axis=1),
        np.concatenate([i_hi, i_lo], axis=1),
        np.stack([b_hi, b_lo]),
        np.stack([v_hi, v_lo]),
        np.stack([np.cos(turn), np.sin(turn)]).astype(np.float32),
    )


def dot(x, y):
    return jnp.dot(x, y, preferred_element_type=f32)


def split(x):
    high = x.astype(bf16)
    return high, (x - high.astype(f32)).astype(bf16)


def rows_of(ref, c):
    return ref[pl.ds(c, NS, stride=CC), :]


def forward(src, a_ref, b_ref, t_ref):
    x = jnp.concatenate([rows_of(src, c) for c in range(CC)], axis=1).astype(bf16)
    a = a_ref[...]
    z = dot(a[:, :NS], x) + dot(a[:, NS:], x)
    tc, ts = t_ref[0], t_ref[1]
    parts = []
    for c in range(CC):
        re = z[:NS, c * TOK : (c + 1) * TOK]
        im = z[NS:, c * TOK : (c + 1) * TOK]
        parts.append(jnp.concatenate([re * tc + im * ts, im * tc - re * ts], axis=1))
    hi, lo = split(jnp.concatenate(parts, axis=0))
    return dot(hi, b_ref[0]) + dot(hi, b_ref[1]) + dot(lo, b_ref[0])


def inverse(spec, i_ref, v_ref, t_ref, dst):
    hi, lo = split(spec)
    v = dot(hi, v_ref[0]) + dot(hi, v_ref[1]) + dot(lo, v_ref[0])
    tc, ts = t_ref[0], t_ref[1]
    parts = []
    for c in range(CC):
        re = v[c * NS : (c + 1) * NS, :TOK]
        im = v[c * NS : (c + 1) * NS, TOK:]
        parts.append(jnp.concatenate([re * tc - im * ts, im * tc + re * ts], axis=0))
    hi, lo = split(jnp.concatenate(parts, axis=1))
    a = i_ref[...]
    y = dot(a[:, : 2 * NS], hi) + dot(a[:, 2 * NS :], hi) + dot(a[:, : 2 * NS], lo)
    for c in range(CC):
        dst[pl.ds(c, NS, stride=CC), :] = y[:, c * TOK : (c + 1) * TOK]


def times(p, q):
    pr, pi, qr, qi = p[:, :TOK], p[:, TOK:], q[:, :TOK], q[:, TOK:]
    return jnp.concatenate([pr * qr - pi * qi, pr * qi + pi * qr], axis=1)


def times_conj(p, q):
    pr, pi, qr, qi = p[:, :TOK], p[:, TOK:], q[:, :TOK], q[:, TOK:]
    return jnp.concatenate([pr * qr + pi * qi, pi * qr - pr * qi], axis=1)


def flat(x):
    return x.reshape(NS * CC, TOK)


def conv_kernel(in_ref, skip_ref, a_ref, i_ref, b_ref, v_ref, t_ref, mixed_ref, gated_ref, sig_ref, tap_ref, buf):
    buf[...] = flat(in_ref[:, 1].astype(f32))
    tap = forward(buf, a_ref, b_ref, t_ref)
    tap_ref[...] = tap
    buf[...] = flat(in_ref[:, 0].astype(f32))
    sig = forward(buf, a_ref, b_ref, t_ref)
    sig_ref[...] = sig
    inverse(times(sig, tap), i_ref, v_ref, t_ref, buf)
    skip = skip_ref[...]
    for n in range(NS):
        mixed = (buf[n * CC : (n + 1) * CC, :] + skip * in_ref[n, 0].astype(f32)).astype(bf16)
        mixed_ref[n] = mixed
        gated = in_ref[n, 2].astype(f32) * mixed.astype(f32)
        z = n % NZ
        gated_ref[n // NZ, :, z * TOK : (z + 1) * TOK] = gated.astype(bf16)


def back_kernel(gg_ref, in_ref, mixed_ref, sig_ref, tap_ref, skip_ref, a_ref, i_ref, b_ref, v_ref, t_ref, out_ref, gs_ref, buf, gmb):
    total = jnp.zeros((CC, TOK), f32)
    for n in range(NS):
        z = n % NZ
        gg = gg_ref[n // NZ, :, z * TOK : (z + 1) * TOK].astype(f32)
        out_ref[n, 2] = (gg * mixed_ref[n].astype(f32)).astype(bf16)
        gm = (gg * in_ref[n, 2].astype(f32)).astype(bf16).astype(f32)
        gmb[n * CC : (n + 1) * CC, :] = gm
        total = total + gm * in_ref[n, 0].astype(f32)
    gs_ref[...] = total * ROOT
    grad = forward(gmb, a_ref, b_ref, t_ref)
    inverse(times_conj(grad, tap_ref[...]), i_ref, v_ref, t_ref, buf)
    skip = skip_ref[...]
    for n in range(NS):
        rows = slice(n * CC, (n + 1) * CC)
        out_ref[n, 0] = (buf[rows, :] + skip * gmb[rows, :]).astype(bf16)
    inverse(times_conj(grad, sig_ref[...]), i_ref, v_ref, t_ref, buf)
    for n in range(NS):
        rows = slice(n * CC, (n + 1) * CC)
        out_ref[n, 1] = (buf[rows, :] * ROOT).astype(bf16)


def whole(array):
    rank = array.ndim
    return pl.BlockSpec(array.shape, lambda i: (0,) * rank)


STEPS = CL // CC
PACK = pl.BlockSpec((NS, 3, CC, TOK), lambda i: (0, 0, i, 0))
PLAIN = pl.BlockSpec((NS, CC, TOK), lambda i: (0, i, 0))
WIDE = pl.BlockSpec((NY, CC, NZ * TOK), lambda i: (0, i, 0))
SPEC = pl.BlockSpec((CC * NS, 2 * TOK), lambda i: (i, 0))
LANE = pl.BlockSpec((CC, TOK), lambda i: (i, 0))
SHAPE = jax.ShapeDtypeStruct


def conv(cols, skip, tabs):
    return pl.pallas_call(
        conv_kernel,
        grid=(STEPS,),
        in_specs=[PACK, LANE] + [whole(t) for t in tabs],
        out_specs=[PLAIN, WIDE, SPEC, SPEC],
        out_shape=[
            SHAPE((NS, CL, TOK), bf16),
            SHAPE((NY, CL, NZ * TOK), bf16),
            SHAPE((CL * NS, 2 * TOK), f32),
            SHAPE((CL * NS, 2 * TOK), f32),
        ],
        scratch_shapes=[pltpu.VMEM((NS * CC, TOK), f32)],
        name="conv",
    )(cols, skip, *tabs)


def back(gg, cols, mixed, sig, tap, skip, tabs):
    return pl.pallas_call(
        back_kernel,
        grid=(STEPS,),
        in_specs=[WIDE, PACK, PLAIN, SPEC, SPEC, LANE] + [whole(t) for t in tabs],
        out_specs=[PACK, LANE],
        out_shape=[SHAPE((NS, 3, CL, TOK), bf16), SHAPE((CL, TOK), f32)],
        scratch_shapes=[pltpu.VMEM((NS * CC, TOK), f32)] * 2,
        name="back",
    )(gg, cols, mixed, sig, tap, skip, *tabs)


def to_cols_kernel(s_ref, f_ref, g_ref, out_ref):
    for i, ref in enumerate((s_ref, f_ref, g_ref)):
        turned = ref[...].astype(f32).T.astype(bf16)
        for j in range(TOK // CL):
            out_ref[j, i] = turned[j * CL : (j + 1) * CL, :]


def to_cols(signal, taps, gate):
    width = signal.shape[1]
    block = pl.BlockSpec((TOK, TOK), lambda i: (0, i))
    return pl.pallas_call(
        to_cols_kernel,
        grid=(width // TOK,),
        in_specs=[block] * 3,
        out_specs=pl.BlockSpec((TOK // CL, 3, CL, TOK), lambda i: (i, 0, 0, 0)),
        out_shape=SHAPE((NS, 3, CL, TOK), bf16),
        name="to_cols",
    )(signal, taps, gate)


def to_rows_kernel(in_ref, a_ref, b_ref, c_ref):
    for i, ref in enumerate((a_ref, b_ref, c_ref)):
        stacked = jnp.concatenate([in_ref[j, i] for j in range(TOK // CL)], axis=0)
        ref[...] = stacked.astype(f32).T.astype(bf16)


def to_rows(cols):
    block = pl.BlockSpec((TOK, TOK), lambda i: (0, i))
    out = SHAPE((TOK, NS * CL), bf16)
    return pl.pallas_call(
        to_rows_kernel,
        grid=(NS * CL // TOK,),
        in_specs=[pl.BlockSpec((TOK // CL, 3, CL, TOK), lambda i: (i, 0, 0, 0))],
        out_specs=[block] * 3,
        out_shape=[out] * 3,
        name="to_rows",
    )(cols)


def gated_kernel(w_ref, cot_ref, out_ref, acc):
    step = pl.program_id(0)
    cot = jnp.concatenate([cot_ref[0], cot_ref[1]], axis=1)
    part = lax.dot_general(w_ref[0], cot, (((1,), (1,)), ((), ())), preferred_element_type=f32)

    @pl.when(step == 0)
    def _():
        acc[...] = part

    @pl.when(jnp.logical_and(step > 0, step < NX - 1))
    def _():
        acc[...] += part

    @pl.when(step == NX - 1)
    def _():
        acc[...] += part
        for y in range(NY):
            for z in range(NZ):
                src = (y * NZ + z) * CL
                out_ref[z, y * CL : (y + 1) * CL, :] = acc[src : src + CL, :].astype(bf16)


def grad_gated_part(w_all, cot_all):
    c, f = w_all.shape[1:]
    t = cot_all.shape[1]
    return pl.pallas_call(
        gated_kernel,
        grid=(NX,),
        in_specs=[
            pl.BlockSpec((1, c, f), lambda i: (i, 0, 0)),
            pl.BlockSpec((NH, t, f // NH), lambda i: (i, 0, 0)),
        ],
        out_specs=pl.BlockSpec((NZ, NY * CL, t), lambda i: (0, 0, 0)),
        out_shape=SHAPE((NZ, NY * CL, t), bf16),
        scratch_shapes=[pltpu.VMEM((c, t), f32)],
        name="grad_gated",
    )(w_all, cot_all)


def weight_kernel(gated_ref, cot_ref, out_ref):
    cot = jnp.concatenate([cot_ref[0], cot_ref[1]], axis=1)
    out_ref[0] = (dot(gated_ref[...], cot) * ROOT).astype(bf16)


def grad_weight_part(gated_all, cot_all):
    c, t = gated_all.shape
    f = NH * cot_all.shape[2]
    return pl.pallas_call(
        weight_kernel,
        grid=(NX,),
        in_specs=[
            pl.BlockSpec((c, t), lambda i: (0, 0)),
            pl.BlockSpec((NH, t, f // NH), lambda i: (i, 0, 0)),
        ],
        out_specs=pl.BlockSpec((1, c, f), lambda i: (i, 0, 0)),
        out_shape=SHAPE((NX, c, f), bf16),
        name="grad_weight",
    )(gated_all, cot_all)


def on_device(signal, gate_values, filter_taps, skip_gain, w_out, cotangent):
    tabs = [jnp.asarray(t) for t in tables()]
    seq, ch = ("y", "z"), ("x", "core")
    w_all = lax.all_gather(w_out, "y", axis=0)
    pieces = cotangent.reshape(TOK, NZ // NH, NH, TOK).transpose(2, 1, 0, 3)
    pieces = lax.all_to_all(pieces, "core", split_axis=0, concat_axis=0, tiled=True)
    pieces = pieces.reshape(NZ, TOK, TOK)
    pieces = lax.all_to_all(pieces, "z", split_axis=0, concat_axis=0, tiled=True)
    cot_all = lax.all_gather(pieces.reshape(NZ * TOK, TOK), ch, axis=0)
    cols = to_cols(signal, filter_taps, gate_values)
    cols = lax.all_to_all(cols, seq, split_axis=0, concat_axis=0, tiled=True)
    skip = jnp.broadcast_to(skip_gain[:, None], (CL, TOK))

    part = grad_gated_part(w_all, cot_all)
    part = lax.all_to_all(part, "z", split_axis=0, concat_axis=0, tiled=True)
    part = jnp.sum(part.astype(f32), axis=0).astype(bf16).reshape(NY, CL, NZ * TOK)

    mixed, gated, sig_spec, tap_spec = conv(cols, skip, tabs)
    gated = lax.all_to_all(gated, "y", split_axis=0, concat_axis=0, tiled=True)
    gated_all = lax.all_gather(gated.reshape(NY * CL, NZ * TOK), "z", axis=0, tiled=True)

    grad_gated = lax.all_to_all(part, "y", split_axis=0, concat_axis=0, tiled=True)
    outs, skip_sum = back(grad_gated, cols, mixed, sig_spec, tap_spec, skip, tabs)
    outs = lax.all_to_all(outs, seq, split_axis=0, concat_axis=0, tiled=True)
    grad_input, grad_filter, grad_gate = to_rows(outs)

    weight = grad_weight_part(gated_all, cot_all)
    weight = lax.psum_scatter(weight, "y", scatter_dimension=0, tiled=True)
    weight = weight.reshape(NZ, NY, CL, -1).transpose(1, 0, 2, 3).reshape(NS * CL, -1)
    return (grad_input, grad_gate, grad_filter, jnp.sum(skip_sum, axis=1), weight.astype(f32))


def solution(mesh):
    fine = Mesh(mesh.devices.reshape(NY, NZ, NX, NH), ("y", "z", "x", "core"))
    seq, ch = ("y", "z"), ("x", "core")
    rows = P(seq, ch)
    vector = P(ch + seq)
    weights = P(ch, seq)
    return jax.shard_map(
        on_device,
        mesh=fine,
        in_specs=(rows, rows, rows, vector, weights, rows),
        out_specs=(rows, rows, rows, vector, weights),
        check_vma=False,
    )
```

```python
import functools
import math

import jax
import jax.numpy as jnp
import numpy as np
from jax import lax
from jax.experimental import pallas as pl
from jax.experimental.pallas import tpu as pltpu
from jax.sharding import Mesh
from jax.sharding import PartitionSpec as P

NY, NZ, NX, NH = 4, 8, 4, 2
NS = NY * NZ
TOK = 128
CL = 32
CC = 16
FREQ = 2 * NS * TOK
ROOT = 1.0 / math.sqrt(NS * TOK)
bf16, f32 = jnp.bfloat16, jnp.float32


def halves(matrix):
    high = matrix.astype(jnp.bfloat16)
    low = (matrix - high.astype(np.float64)).astype(jnp.bfloat16)
    return high, low


def tables():
    k = np.arange(NS)[:, None] + 0.5
    n = np.arange(NS)[None, :]
    m = np.arange(TOK)[None, :]
    outer = 2.0 * np.pi * k * n / (2 * NS)
    a = np.concatenate([np.cos(outer), -np.sin(outer)], axis=0)
    a_inv = np.concatenate([np.cos(outer).T, -np.sin(outer).T], axis=1) * (2.0 / FREQ)
    turn = 2.0 * np.pi * k * m / FREQ
    inner = 2.0 * np.pi * (np.arange(TOK)[:, None] * m % TOK) / TOK
    c, s = np.cos(inner), np.sin(inner)
    b = np.block([[c, -s], [s, c]])
    b_inv = np.block([[c, s], [-s, c]])
    a_hi, a_lo = halves(a)
    i_hi, i_lo = halves(a_inv)
    b_hi, b_lo = halves(b)
    v_hi, v_lo = halves(b_inv)
    return (
        np.concatenate([a_hi, a_lo], axis=1),
        np.concatenate([i_hi, i_lo], axis=1),
        np.stack([b_hi, b_lo]),
        np.stack([v_hi, v_lo]),
        np.stack([np.cos(turn), np.sin(turn)]).astype(np.float32),
    )


def dot(x, y):
    return jnp.dot(x, y, preferred_element_type=f32)


def split(x):
    high = x.astype(bf16)
    return high, (x - high.astype(f32)).astype(bf16)


def rows_of(ref, c):
    return ref[pl.ds(c, NS, stride=CC), :]


def forward(src, a_ref, b_ref, t_ref):
    x = jnp.concatenate([rows_of(src, c) for c in range(CC)], axis=1).astype(bf16)
    a = a_ref[...]
    z = dot(a[:, :NS], x) + dot(a[:, NS:], x)
    tc, ts = t_ref[0], t_ref[1]
    parts = []
    for c in range(CC):
        re = z[:NS, c * TOK : (c + 1) * TOK]
        im = z[NS:, c * TOK : (c + 1) * TOK]
        parts.append(jnp.concatenate([re * tc + im * ts, im * tc - re * ts], axis=1))
    hi, lo = split(jnp.concatenate(parts, axis=0))
    return dot(hi, b_ref[0]) + dot(hi, b_ref[1]) + dot(lo, b_ref[0])


def inverse(spec, i_ref, v_ref, t_ref, dst):
    hi, lo = split(spec)
    v = dot(hi, v_ref[0]) + dot(hi, v_ref[1]) + dot(lo, v_ref[0])
    tc, ts = t_ref[0], t_ref[1]
    parts = []
    for c in range(CC):
        re = v[c * NS : (c + 1) * NS, :TOK]
        im = v[c * NS : (c + 1) * NS, TOK:]
        parts.append(jnp.concatenate([re * tc - im * ts, im * tc + re * ts], axis=0))
    hi, lo = split(jnp.concatenate(parts, axis=1))
    a = i_ref[...]
    y = dot(a[:, : 2 * NS], hi) + dot(a[:, 2 * NS :], hi) + dot(a[:, : 2 * NS], lo)
    for c in range(CC):
        dst[pl.ds(c, NS, stride=CC), :] = y[:, c * TOK : (c + 1) * TOK]


def times(p, q):
    pr, pi, qr, qi = p[:, :TOK], p[:, TOK:], q[:, :TOK], q[:, TOK:]
    return jnp.concatenate([pr * qr - pi * qi, pr * qi + pi * qr], axis=1)


def times_conj(p, q):
    pr, pi, qr, qi = p[:, :TOK], p[:, TOK:], q[:, :TOK], q[:, TOK:]
    return jnp.concatenate([pr * qr + pi * qi, pi * qr - pr * qi], axis=1)


def flat(x):
    return x.reshape(NS * CC, TOK)


def conv_kernel(in_ref, skip_ref, a_ref, i_ref, b_ref, v_ref, t_ref, mixed_ref, gated_ref, sig_ref, tap_ref, buf):
    buf[...] = flat(in_ref[:, 1].astype(f32))
    tap = forward(buf, a_ref, b_ref, t_ref)
    tap_ref[...] = tap
    buf[...] = flat(in_ref[:, 0].astype(f32))
    sig = forward(buf, a_ref, b_ref, t_ref)
    sig_ref[...] = sig
    inverse(times(sig, tap), i_ref, v_ref, t_ref, buf)
    skip = skip_ref[...]
    for n in range(NS):
        mixed = (buf[n * CC : (n + 1) * CC, :] + skip * in_ref[n, 0].astype(f32)).astype(bf16)
        mixed_ref[n] = mixed
        gated = in_ref[n, 2].astype(f32) * mixed.astype(f32)
        z = n % NZ
        gated_ref[n // NZ, :, z * TOK : (z + 1) * TOK] = gated.astype(bf16)


def back_kernel(gg_ref, in_ref, mixed_ref, sig_ref, tap_ref, skip_ref, a_ref, i_ref, b_ref, v_ref, t_ref, out_ref, gs_ref, buf, gmb):
    total = jnp.zeros((CC, TOK), f32)
    for n in range(NS):
        z = n % NZ
        gg = gg_ref[n // NZ, :, z * TOK : (z + 1) * TOK].astype(f32)
        out_ref[n, 2] = (gg * mixed_ref[n].astype(f32)).astype(bf16)
        gm = (gg * in_ref[n, 2].astype(f32)).astype(bf16).astype(f32)
        gmb[n * CC : (n + 1) * CC, :] = gm
        total = total + gm * in_ref[n, 0].astype(f32)
    gs_ref[...] = total * ROOT
    grad = forward(gmb, a_ref, b_ref, t_ref)
    inverse(times_conj(grad, tap_ref[...]), i_ref, v_ref, t_ref, buf)
    skip = skip_ref[...]
    for n in range(NS):
        rows = slice(n * CC, (n + 1) * CC)
        out_ref[n, 0] = (buf[rows, :] + skip * gmb[rows, :]).astype(bf16)
    inverse(times_conj(grad, sig_ref[...]), i_ref, v_ref, t_ref, buf)
    for n in range(NS):
        rows = slice(n * CC, (n + 1) * CC)
        out_ref[n, 1] = (buf[rows, :] * ROOT).astype(bf16)


def whole(array):
    rank = array.ndim
    return pl.BlockSpec(array.shape, lambda i: (0,) * rank)


STEPS = CL // CC
PACK = pl.BlockSpec((NS, 3, CC, TOK), lambda i: (0, 0, i, 0))
PLAIN = pl.BlockSpec((NS, CC, TOK), lambda i: (0, i, 0))
WIDE = pl.BlockSpec((NY, CC, NZ * TOK), lambda i: (0, i, 0))
SPEC = pl.BlockSpec((CC * NS, 2 * TOK), lambda i: (i, 0))
LANE = pl.BlockSpec((CC, TOK), lambda i: (i, 0))
SHAPE = jax.ShapeDtypeStruct


def conv(cols, skip, tabs):
    return pl.pallas_call(
        conv_kernel,
        grid=(STEPS,),
        in_specs=[PACK, LANE] + [whole(t) for t in tabs],
        out_specs=[PLAIN, WIDE, SPEC, SPEC],
        out_shape=[
            SHAPE((NS, CL, TOK), bf16),
            SHAPE((NY, CL, NZ * TOK), bf16),
            SHAPE((CL * NS, 2 * TOK), f32),
            SHAPE((CL * NS, 2 * TOK), f32),
        ],
        scratch_shapes=[pltpu.VMEM((NS * CC, TOK), f32)],
        name="conv",
    )(cols, skip, *tabs)


def back(gg, cols, mixed, sig, tap, skip, tabs):
    return pl.pallas_call(
        back_kernel,
        grid=(STEPS,),
        in_specs=[WIDE, PACK, PLAIN, SPEC, SPEC, LANE] + [whole(t) for t in tabs],
        out_specs=[PACK, LANE],
        out_shape=[SHAPE((NS, 3, CL, TOK), bf16), SHAPE((CL, TOK), f32)],
        scratch_shapes=[pltpu.VMEM((NS * CC, TOK), f32)] * 2,
        name="back",
    )(gg, cols, mixed, sig, tap, skip, *tabs)


def to_cols_kernel(s_ref, f_ref, g_ref, out_ref):
    for i, ref in enumerate((s_ref, f_ref, g_ref)):
        for b in range(ref.shape[1] // TOK):
            turned = ref[:, b * TOK : (b + 1) * TOK].T
            for j in range(TOK // CL):
                out_ref[b * (TOK // CL) + j, i] = turned[j * CL : (j + 1) * CL, :]


def to_cols(signal, taps, gate):
    width = signal.shape[1]
    span = 4 * TOK
    block = pl.BlockSpec((TOK, span), lambda i: (0, i))
    return pl.pallas_call(
        to_cols_kernel,
        grid=(width // span,),
        in_specs=[block] * 3,
        out_specs=pl.BlockSpec((span // CL, 3, CL, TOK), lambda i: (i, 0, 0, 0)),
        out_shape=SHAPE((NS, 3, CL, TOK), bf16),
        name="to_cols",
    )(signal, taps, gate)


def to_rows_kernel(in_ref, a_ref, b_ref, c_ref):
    for i, ref in enumerate((a_ref, b_ref, c_ref)):
        for b in range(ref.shape[1] // TOK):
            first = b * (TOK // CL)
            stacked = jnp.concatenate([in_ref[first + j, i] for j in range(TOK // CL)], axis=0)
            ref[:, b * TOK : (b + 1) * TOK] = stacked.T


def to_rows(cols):
    span = 4 * TOK
    block = pl.BlockSpec((TOK, span), lambda i: (0, i))
    out = SHAPE((TOK, NS * CL), bf16)
    return pl.pallas_call(
        to_rows_kernel,
        grid=(NS * CL // span,),
        in_specs=[pl.BlockSpec((span // CL, 3, CL, TOK), lambda i: (i, 0, 0, 0))],
        out_specs=[block] * 3,
        out_shape=[out] * 3,
        name="to_rows",
    )(cols)


OWN = (3, 2, 1, 6, 7, 0)
SENT = (4, 5)


def gated_kernel(at, w0, w1, w2, w3, q0, q1, q2, q3, cot_ref, own_ref, sent_ref, acc):
    y, z, x, core = at[0], at[1], at[2], at[3]
    for s, q in enumerate((q0, q1, q2, q3)):
        mine, other = q[0], q[1]
        first = jnp.where(core == 0, mine, other)
        second = jnp.where(core == 0, other, mine)
        cot_ref[(x + s) % NX] = jnp.concatenate([first, second], axis=1)
    total = None
    for r, w in enumerate((w0, w1, w2, w3)):
        part = lax.dot_general(
            w[...], cot_ref[(y + r) % NY], (((1,), (1,)), ((), ())), preferred_element_type=f32
        )
        total = part if total is None else total + part
    acc[...] = total

    def block(offset, b):
        return acc[pl.ds(pl.multiple_of((b * NZ + (z + offset) % NZ) * CL, CL), CL), :]

    for b in range(NY):
        rows = slice(b * CL, (b + 1) * CL)
        for i, offset in enumerate(OWN):
            own_ref[i, rows, :] = block(offset, b)
        for i, offset in enumerate(SENT):
            sent_ref[i, rows, :] = block(offset, b).astype(bf16)


def grad_gated_part(at, ws, qs):
    c, f = ws[0].shape
    t = qs[0].shape[1]
    span = 2 * TOK
    return pl.pallas_call(
        gated_kernel,
        grid_spec=pltpu.PrefetchScalarGridSpec(
            num_scalar_prefetch=1,
            grid=(t // span,),
            in_specs=[pl.BlockSpec((c, f), lambda i, at: (0, 0))] * NY
            + [pl.BlockSpec((NH, span, f // NH), lambda i, at: (0, i, 0))] * NX,
            out_specs=[
                pl.BlockSpec((NX, span, f), lambda i, at: (0, i, 0)),
                pl.BlockSpec((len(OWN), NY * CL, span), lambda i, at: (0, 0, i)),
                pl.BlockSpec((len(SENT), NY * CL, span), lambda i, at: (0, 0, i)),
            ],
            scratch_shapes=[pltpu.VMEM((c, span), f32)],
        ),
        out_shape=[
            SHAPE((NX, t, f), bf16),
            SHAPE((len(OWN), NY * CL, t), f32),
            SHAPE((len(SENT), NY * CL, t), bf16),
        ],
        name="grad_gated",
    )(at, *ws, *qs)


def weight_kernel(at, *refs):
    pieces, cot_ref, outs, gated = refs[: NZ + 1], refs[NZ + 1], refs[NZ + 2 : -1], refs[-1]
    step = pl.program_id(0)

    @pl.when(step == 0)
    def _():
        row = 0
        for piece in pieces:
            gated[row : row + piece.shape[0], :] = piece[...]
            row += piece.shape[0]

    part = (dot(gated[...], cot_ref[0]) * ROOT).astype(bf16)
    for i, out in enumerate(outs):

        @pl.when(step == i)
        def _():
            out[...] = part


def grad_weight_part(at, pieces, cot_all):
    c, t, f = NS * CL, cot_all.shape[1], cot_all.shape[2]
    return pl.pallas_call(
        weight_kernel,
        grid_spec=pltpu.PrefetchScalarGridSpec(
            num_scalar_prefetch=1,
            grid=(NY,),
            in_specs=[pl.BlockSpec(p.shape, lambda i, at: (0, 0)) for p in pieces]
            + [pl.BlockSpec((1, t, f), lambda i, at: ((at[0] + i) % NY, 0, 0))],
            out_specs=[pl.BlockSpec((c, f), lambda i, at: (0, 0))] * NY,
            scratch_shapes=[pltpu.VMEM((c, t), bf16)],
        ),
        out_shape=[SHAPE((c, f), bf16)] * NY,
        name="grad_weight",
    )(at, *pieces, cot_all)


def sum_kernel(at, a_ref, b_ref, c_ref, d_ref, out_ref):
    total = a_ref[...].astype(f32) + b_ref[...].astype(f32) + c_ref[...].astype(f32) + d_ref[...].astype(f32)
    for b in range(NY):
        out_ref[b, 0] = total[b * CL : (b + 1) * CL, :]


def weight_sum(at, parts):
    c, f = parts[0].shape
    return pl.pallas_call(
        sum_kernel,
        grid_spec=pltpu.PrefetchScalarGridSpec(
            num_scalar_prefetch=1,
            grid=(NZ,),
            in_specs=[pl.BlockSpec((c // NZ, f), lambda i, at: (i, 0))] * NY,
            out_specs=pl.BlockSpec((NY, 1, CL, f), lambda i, at: (0, (at[1] + i) % NZ, 0, 0)),
        ),
        out_shape=SHAPE((NY, NZ, CL, f), f32),
        name="weight_sum",
    )(at, *parts).reshape(c, f)


def shift(value, axis, by):
    count = lax.axis_size(axis)
    return lax.ppermute(value, axis, [(i, (i + by) % count) for i in range(count)])


def add(received, own):
    return (received.astype(f32) + own).astype(bf16)


def on_device(signal, gate_values, filter_taps, skip_gain, w_out, cotangent):
    tabs = [jnp.asarray(t) for t in tables()]
    seq = ("y", "z")
    at = jnp.stack([lax.axis_index(a) for a in ("y", "z", "x", "core")]).astype(jnp.int32)
    ws = [w_out, shift(w_out, "y", -1), shift(w_out, "y", 2), shift(w_out, "y", 1)]

    pieces = cotangent.reshape(TOK, NZ // NH, NH, TOK).transpose(2, 1, 0, 3)
    pieces = lax.all_to_all(pieces, "core", split_axis=0, concat_axis=0, tiled=True)
    pieces = pieces.reshape(NZ, TOK, TOK)
    pieces = lax.all_to_all(pieces, "z", split_axis=0, concat_axis=0, tiled=True)
    pieces = pieces.reshape(NZ * TOK, TOK)
    chip = jnp.stack([pieces, shift(pieces, "core", 1)])
    chips = [chip, shift(chip, "x", -1), shift(chip, "x", 2), shift(chip, "x", 1)]

    cols = to_cols(signal, filter_taps, gate_values)
    cols = lax.all_to_all(cols, seq, split_axis=0, concat_axis=0, tiled=True)
    skip = jnp.broadcast_to(skip_gain[:, None], (CL, TOK))

    cot_all, own, sent = grad_gated_part(at, ws, chips)
    up = shift(sent[0], "z", 1)
    down = shift(sent[1], "z", -1)

    mixed, gated, sig_spec, tap_spec = conv(cols, skip, tabs)
    gated = lax.all_to_all(gated, "y", split_axis=0, concat_axis=0, tiled=True)
    gated = gated.reshape(NY * CL, NZ * TOK)

    for i in range(2):
        up = shift(add(up, own[i]), "z", 1)
        down = shift(add(down, own[3 + i]), "z", -1)
    up = shift(add(up, own[2]), "z", 1)
    part = (up.astype(f32) + down.astype(f32) + own[5]).astype(bf16)

    before, after = [gated], [gated]
    for _ in range(3):
        before.append(shift(before[-1], "z", 1))
        after.append(shift(after[-1], "z", -1))
    half = NY * CL // 2
    far = [shift(before[-1][:half], "z", 1), shift(after[-1][half:], "z", -1)]
    ring = [gated] + after[1:] + far + before[:0:-1]

    part = part.reshape(NY, CL, NZ * TOK)
    grad_gated = lax.all_to_all(part, "y", split_axis=0, concat_axis=0, tiled=True)
    outs, skip_sum = back(grad_gated, cols, mixed, sig_spec, tap_spec, skip, tabs)
    outs = lax.all_to_all(outs, seq, split_axis=0, concat_axis=0, tiled=True)
    grad_input, grad_filter, grad_gate = to_rows(outs)

    kept, up1, up2, up3 = grad_weight_part(at, ring, cot_all)
    weight = weight_sum(at, [kept, shift(up1, "y", 1), shift(up2, "y", 2), shift(up3, "y", -1)])
    return (grad_input, grad_gate, grad_filter, jnp.sum(skip_sum, axis=1), weight)


def solution(mesh):
    fine = Mesh(mesh.devices.reshape(NY, NZ, NX, NH), ("y", "z", "x", "core"))
    seq, ch = ("y", "z"), ("x", "core")
    rows = P(seq, ch)
    vector = P(ch + seq)
    weights = P(ch, seq)
    return jax.shard_map(
        on_device,
        mesh=fine,
        in_specs=(rows, rows, rows, vector, weights, rows),
        out_specs=(rows, rows, rows, vector, weights),
        check_vma=False,
    )
```

```python
import math

import jax
import jax.numpy as jnp
import numpy as np
from jax import lax
from jax.experimental import pallas as pl
from jax.experimental.pallas import tpu as pltpu
from jax.sharding import Mesh
from jax.sharding import PartitionSpec as P

NY, NZ, NX, NH = 4, 8, 4, 2
NS = NY * NZ
TOK = 128
CL = 32
CC = 16
FREQ = 2 * NS * TOK
ROOT = 1.0 / math.sqrt(NS * TOK)
bf16, f32 = jnp.bfloat16, jnp.float32


def halves(matrix):
    high = matrix.astype(jnp.bfloat16)
    low = (matrix - high.astype(np.float64)).astype(jnp.bfloat16)
    return high, low


def tables():
    k = np.arange(NS)[:, None] + 0.5
    n = np.arange(NS)[None, :]
    m = np.arange(TOK)[None, :]
    outer = 2.0 * np.pi * k * n / (2 * NS)
    a = np.concatenate([np.cos(outer), -np.sin(outer)], axis=0)
    a_inv = np.concatenate([np.cos(outer).T, -np.sin(outer).T], axis=1) * (2.0 / FREQ)
    turn = 2.0 * np.pi * k * m / FREQ
    inner = 2.0 * np.pi * (np.arange(TOK)[:, None] * m % TOK) / TOK
    c, s = np.cos(inner), np.sin(inner)
    b = np.block([[c, -s], [s, c]])
    b_inv = np.block([[c, s], [-s, c]])
    a_hi, a_lo = halves(a)
    i_hi, i_lo = halves(a_inv)
    b_hi, b_lo = halves(b)
    v_hi, v_lo = halves(b_inv)
    return (
        np.concatenate([a_hi, a_lo], axis=1),
        np.concatenate([i_hi, i_lo], axis=1),
        np.stack([b_hi, b_lo]),
        np.stack([v_hi, v_lo]),
        np.stack([np.cos(turn), np.sin(turn)]).astype(np.float32),
    )


def dot(x, y):
    return jnp.dot(x, y, preferred_element_type=f32)


def split(x):
    high = x.astype(bf16)
    return high, (x - high.astype(f32)).astype(bf16)


def rows_of(ref, c):
    return ref[pl.ds(c, NS, stride=CC), :]


def forward(src, a_ref, b_ref, t_ref):
    x = jnp.concatenate([rows_of(src, c) for c in range(CC)], axis=1).astype(bf16)
    a = a_ref[...]
    z = dot(a[:, :NS], x) + dot(a[:, NS:], x)
    tc, ts = t_ref[0], t_ref[1]
    parts = []
    for c in range(CC):
        re = z[:NS, c * TOK : (c + 1) * TOK]
        im = z[NS:, c * TOK : (c + 1) * TOK]
        parts.append(jnp.concatenate([re * tc + im * ts, im * tc - re * ts], axis=1))
    hi, lo = split(jnp.concatenate(parts, axis=0))
    return dot(hi, b_ref[0]) + dot(hi, b_ref[1]) + dot(lo, b_ref[0])


def inverse(spec, i_ref, v_ref, t_ref, dst):
    hi, lo = split(spec)
    v = dot(hi, v_ref[0]) + dot(hi, v_ref[1]) + dot(lo, v_ref[0])
    tc, ts = t_ref[0], t_ref[1]
    parts = []
    for c in range(CC):
        re = v[c * NS : (c + 1) * NS, :TOK]
        im = v[c * NS : (c + 1) * NS, TOK:]
        parts.append(jnp.concatenate([re * tc - im * ts, im * tc + re * ts], axis=0))
    hi, lo = split(jnp.concatenate(parts, axis=1))
    a = i_ref[...]
    y = dot(a[:, : 2 * NS], hi) + dot(a[:, 2 * NS :], hi) + dot(a[:, : 2 * NS], lo)
    for c in range(CC):
        dst[pl.ds(c, NS, stride=CC), :] = y[:, c * TOK : (c + 1) * TOK]


def times(p, q):
    pr, pi, qr, qi = p[:, :TOK], p[:, TOK:], q[:, :TOK], q[:, TOK:]
    return jnp.concatenate([pr * qr - pi * qi, pr * qi + pi * qr], axis=1)


def times_conj(p, q):
    pr, pi, qr, qi = p[:, :TOK], p[:, TOK:], q[:, :TOK], q[:, TOK:]
    return jnp.concatenate([pr * qr + pi * qi, pi * qr - pr * qi], axis=1)


def flat(x):
    return x.reshape(NS * CC, TOK)


def conv_kernel(in_ref, skip_ref, a_ref, i_ref, b_ref, v_ref, t_ref, mixed_ref, gated_ref, sig_ref, tap_ref, buf):
    buf[...] = flat(in_ref[:, 1].astype(f32))
    tap = forward(buf, a_ref, b_ref, t_ref)
    tap_ref[...] = tap
    buf[...] = flat(in_ref[:, 0].astype(f32))
    sig = forward(buf, a_ref, b_ref, t_ref)
    sig_ref[...] = sig
    inverse(times(sig, tap), i_ref, v_ref, t_ref, buf)
    skip = skip_ref[...]
    for n in range(NS):
        mixed = (buf[n * CC : (n + 1) * CC, :] + skip * in_ref[n, 0].astype(f32)).astype(bf16)
        mixed_ref[n] = mixed
        gated = in_ref[n, 2].astype(f32) * mixed.astype(f32)
        z = n % NZ
        gated_ref[n // NZ, :, z * TOK : (z + 1) * TOK] = gated.astype(bf16)


def back_kernel(gg_ref, in_ref, mixed_ref, sig_ref, tap_ref, skip_ref, a_ref, i_ref, b_ref, v_ref, t_ref, out_ref, gs_ref, buf, gmb):
    total = jnp.zeros((CC, TOK), f32)
    for n in range(NS):
        z = n % NZ
        gg = gg_ref[n // NZ, :, z * TOK : (z + 1) * TOK].astype(f32)
        out_ref[n, 2] = (gg * mixed_ref[n].astype(f32)).astype(bf16)
        gm = (gg * in_ref[n, 2].astype(f32)).astype(bf16).astype(f32)
        gmb[n * CC : (n + 1) * CC, :] = gm
        total = total + gm * in_ref[n, 0].astype(f32)
    gs_ref[...] = total * ROOT
    grad = forward(gmb, a_ref, b_ref, t_ref)
    inverse(times_conj(grad, tap_ref[...]), i_ref, v_ref, t_ref, buf)
    skip = skip_ref[...]
    for n in range(NS):
        rows = slice(n * CC, (n + 1) * CC)
        out_ref[n, 0] = (buf[rows, :] + skip * gmb[rows, :]).astype(bf16)
    inverse(times_conj(grad, sig_ref[...]), i_ref, v_ref, t_ref, buf)
    for n in range(NS):
        rows = slice(n * CC, (n + 1) * CC)
        out_ref[n, 1] = (buf[rows, :] * ROOT).astype(bf16)


def whole(array):
    rank = array.ndim
    return pl.BlockSpec(array.shape, lambda i: (0,) * rank)


STEPS = CL // CC
PACK = pl.BlockSpec((NS, 3, CC, TOK), lambda i: (0, 0, i, 0))
PLAIN = pl.BlockSpec((NS, CC, TOK), lambda i: (0, i, 0))
WIDE = pl.BlockSpec((NY, CC, NZ * TOK), lambda i: (0, i, 0))
SPEC = pl.BlockSpec((CC * NS, 2 * TOK), lambda i: (i, 0))
LANE = pl.BlockSpec((CC, TOK), lambda i: (i, 0))
SHAPE = jax.ShapeDtypeStruct


def conv(cols, skip, tabs):
    return pl.pallas_call(
        conv_kernel,
        grid=(STEPS,),
        in_specs=[PACK, LANE] + [whole(t) for t in tabs],
        out_specs=[PLAIN, WIDE, SPEC, SPEC],
        out_shape=[
            SHAPE((NS, CL, TOK), bf16),
            SHAPE((NY, CL, NZ * TOK), bf16),
            SHAPE((CL * NS, 2 * TOK), f32),
            SHAPE((CL * NS, 2 * TOK), f32),
        ],
        scratch_shapes=[pltpu.VMEM((NS * CC, TOK), f32)],
        name="conv",
    )(cols, skip, *tabs)


def back(gg, cols, mixed, sig, tap, skip, tabs):
    return pl.pallas_call(
        back_kernel,
        grid=(STEPS,),
        in_specs=[WIDE, PACK, PLAIN, SPEC, SPEC, LANE] + [whole(t) for t in tabs],
        out_specs=[PACK, LANE],
        out_shape=[SHAPE((NS, 3, CL, TOK), bf16), SHAPE((CL, TOK), f32)],
        scratch_shapes=[pltpu.VMEM((NS * CC, TOK), f32)] * 2,
        name="back",
    )(gg, cols, mixed, sig, tap, skip, *tabs)


def to_cols_kernel(s_ref, f_ref, g_ref, out_ref):
    for i, ref in enumerate((s_ref, f_ref, g_ref)):
        for b in range(ref.shape[1] // TOK):
            turned = ref[:, b * TOK : (b + 1) * TOK].T
            for j in range(TOK // CL):
                out_ref[b * (TOK // CL) + j, i] = turned[j * CL : (j + 1) * CL, :]


def to_cols(signal, taps, gate):
    width = signal.shape[1]
    span = 4 * TOK
    block = pl.BlockSpec((TOK, span), lambda i: (0, i))
    return pl.pallas_call(
        to_cols_kernel,
        grid=(width // span,),
        in_specs=[block] * 3,
        out_specs=pl.BlockSpec((span // CL, 3, CL, TOK), lambda i: (i, 0, 0, 0)),
        out_shape=SHAPE((NS, 3, CL, TOK), bf16),
        name="to_cols",
    )(signal, taps, gate)


def to_rows_kernel(in_ref, a_ref, b_ref, c_ref):
    for i, ref in enumerate((a_ref, b_ref, c_ref)):
        for b in range(ref.shape[1] // TOK):
            first = b * (TOK // CL)
            stacked = jnp.concatenate([in_ref[first + j, i] for j in range(TOK // CL)], axis=0)
            ref[:, b * TOK : (b + 1) * TOK] = stacked.T


def to_rows(cols):
    span = 4 * TOK
    block = pl.BlockSpec((TOK, span), lambda i: (0, i))
    out = SHAPE((TOK, NS * CL), bf16)
    return pl.pallas_call(
        to_rows_kernel,
        grid=(NS * CL // span,),
        in_specs=[pl.BlockSpec((span // CL, 3, CL, TOK), lambda i: (i, 0, 0, 0))],
        out_specs=[block] * 3,
        out_shape=[out] * 3,
        name="to_rows",
    )(cols)


OWN = (3, 2, 1, 6, 7, 0)
SENT = (4, 5)


def gated_kernel(at, w0, w1, w2, w3, q0, q1, q2, q3, cot_ref, own_ref, sent_ref, acc):
    y, z, x, core = at[0], at[1], at[2], at[3]
    for s, q in enumerate((q0, q1, q2, q3)):
        mine, other = q[0], q[1]
        first = jnp.where(core == 0, mine, other)
        second = jnp.where(core == 0, other, mine)
        cot_ref[(x + s) % NX] = jnp.concatenate([first, second], axis=1)
    total = None
    for r, w in enumerate((w0, w1, w2, w3)):
        part = lax.dot_general(
            w[...], cot_ref[(y + r) % NY], (((1,), (1,)), ((), ())), preferred_element_type=f32
        )
        total = part if total is None else total + part
    acc[...] = total

    def block(offset, b):
        return acc[pl.ds(pl.multiple_of((b * NZ + (z + offset) % NZ) * CL, CL), CL), :]

    for b in range(NY):
        rows = slice(b * CL, (b + 1) * CL)
        for i, offset in enumerate(OWN):
            own_ref[i, rows, :] = block(offset, b)
        for i, offset in enumerate(SENT):
            sent_ref[i, rows, :] = block(offset, b).astype(bf16)


def grad_gated_part(at, ws, qs):
    c, f = ws[0].shape
    t = qs[0].shape[1]
    span = 2 * TOK
    return pl.pallas_call(
        gated_kernel,
        grid_spec=pltpu.PrefetchScalarGridSpec(
            num_scalar_prefetch=1,
            grid=(t // span,),
            in_specs=[pl.BlockSpec((c, f), lambda i, at: (0, 0))] * NY
            + [pl.BlockSpec((NH, span, f // NH), lambda i, at: (0, i, 0))] * NX,
            out_specs=[
                pl.BlockSpec((NX, span, f), lambda i, at: (0, i, 0)),
                pl.BlockSpec((len(OWN), NY * CL, span), lambda i, at: (0, 0, i)),
                pl.BlockSpec((len(SENT), NY * CL, span), lambda i, at: (0, 0, i)),
            ],
            scratch_shapes=[pltpu.VMEM((c, span), f32)],
        ),
        out_shape=[
            SHAPE((NX, t, f), bf16),
            SHAPE((len(OWN), NY * CL, t), f32),
            SHAPE((len(SENT), NY * CL, t), bf16),
        ],
        name="grad_gated",
    )(at, *ws, *qs)


def weight_kernel(at, *refs):
    pieces, cot_ref, outs, gated = refs[: NZ + 1], refs[NZ + 1], refs[NZ + 2 : -1], refs[-1]
    step = pl.program_id(0)

    @pl.when(step == 0)
    def _():
        row = 0
        for piece in pieces:
            gated[row : row + piece.shape[0], :] = piece[...]
            row += piece.shape[0]

    part = (dot(gated[...], cot_ref[0]) * ROOT).astype(bf16)
    for i, out in enumerate(outs):

        @pl.when(step == i)
        def _():
            out[...] = part


def grad_weight_part(at, pieces, cot_all):
    c, t, f = NS * CL, cot_all.shape[1], cot_all.shape[2]
    return pl.pallas_call(
        weight_kernel,
        grid_spec=pltpu.PrefetchScalarGridSpec(
            num_scalar_prefetch=1,
            grid=(NY,),
            in_specs=[pl.BlockSpec(p.shape, lambda i, at: (0, 0)) for p in pieces]
            + [pl.BlockSpec((1, t, f), lambda i, at: ((at[0] + i) % NY, 0, 0))],
            out_specs=[pl.BlockSpec((c, f), lambda i, at: (0, 0))] * NY,
            scratch_shapes=[pltpu.VMEM((c, t), bf16)],
        ),
        out_shape=[SHAPE((c, f), bf16)] * NY,
        name="grad_weight",
    )(at, *pieces, cot_all)


def sum_kernel(at, a_ref, b_ref, c_ref, d_ref, out_ref):
    z = at[1]
    for r in range(NZ):
        for b in range(NY):
            rows = slice((r * NY + b) * CL, (r * NY + b + 1) * CL)
            total = a_ref[rows, :].astype(f32) + b_ref[rows, :].astype(f32)
            total = total + c_ref[rows, :].astype(f32) + d_ref[rows, :].astype(f32)
            out_ref[b, (z + r) % NZ] = total


def weight_sum(at, parts):
    c, f = parts[0].shape
    return pl.pallas_call(
        sum_kernel,
        grid_spec=pltpu.PrefetchScalarGridSpec(
            num_scalar_prefetch=1,
            grid=(f // TOK,),
            in_specs=[pl.BlockSpec((c, TOK), lambda i, at: (0, i))] * NY,
            out_specs=pl.BlockSpec((NY, NZ, CL, TOK), lambda i, at: (0, 0, 0, i)),
        ),
        out_shape=SHAPE((NY, NZ, CL, f), f32),
        name="weight_sum",
    )(at, *parts).reshape(c, f)


def shift(value, axis, by):
    count = lax.axis_size(axis)
    return lax.ppermute(value, axis, [(i, (i + by) % count) for i in range(count)])


def add(received, own):
    return (received.astype(f32) + own).astype(bf16)


def after(value, *earlier):
    return lax.optimization_barrier((value,) + earlier)[0]


def ordered(signal, gate_values, filter_taps, skip_gain, w_out, cotangent):
    tabs = [jnp.asarray(t) for t in tables()]
    seq = ("y", "z")
    at = jnp.stack([lax.axis_index(a) for a in ("y", "z", "x", "core")]).astype(jnp.int32)
    ws = [w_out, shift(w_out, "y", -1), shift(w_out, "y", 2), shift(w_out, "y", 1)]

    pieces = cotangent.reshape(TOK, NZ // NH, NH, TOK).transpose(2, 1, 0, 3)
    pieces = lax.all_to_all(pieces, "core", split_axis=0, concat_axis=0, tiled=True)
    pieces = pieces.reshape(NZ, TOK, TOK)
    pieces = lax.all_to_all(pieces, "z", split_axis=0, concat_axis=0, tiled=True)
    pieces = pieces.reshape(NZ * TOK, TOK)
    chip = jnp.stack([pieces, shift(pieces, "core", 1)])
    chips = [chip, shift(chip, "x", -1), shift(chip, "x", 2), shift(chip, "x", 1)]

    cols = to_cols(after(signal, pieces), filter_taps, gate_values)
    cols = lax.all_to_all(cols, seq, split_axis=0, concat_axis=0, tiled=True)

    cot_all, own, sent = grad_gated_part(after(at, cols), ws, chips)
    up = shift(sent[0], "z", 1)
    down = shift(sent[1], "z", -1)

    skip = jnp.broadcast_to(after(skip_gain, own)[:, None], (CL, TOK))
    mixed, gated, sig_spec, tap_spec = conv(cols, skip, tabs)
    gated = lax.all_to_all(gated, "y", split_axis=0, concat_axis=0, tiled=True)
    gated = gated.reshape(NY * CL, NZ * TOK)

    for i in range(2):
        up, down = lax.optimization_barrier((up, down))
        up, down = add(up, own[i]), add(down, own[3 + i])
        up = shift(up, "z", 1)
        down = shift(down, "z", -1)
    up, down = lax.optimization_barrier((up, down))
    rest = down.astype(f32) + own[5]
    up = shift(add(up, own[2]), "z", 1)
    part = (up.astype(f32) + rest).astype(bf16)

    fore, aft = [gated], [gated]
    for _ in range(3):
        fore.append(shift(fore[-1], "z", 1))
        aft.append(shift(aft[-1], "z", -1))
    half = NY * CL // 2
    far = [shift(fore[-1][:half], "z", 1), shift(aft[-1][half:], "z", -1)]
    ring = [gated] + aft[1:] + far + fore[:0:-1]

    part = part.reshape(NY, CL, NZ * TOK)
    grad_gated = lax.all_to_all(part, "y", split_axis=0, concat_axis=0, tiled=True)
    outs, skip_sum = back(grad_gated, cols, mixed, sig_spec, tap_spec, skip, tabs)
    outs_rows = lax.all_to_all(outs, seq, split_axis=0, concat_axis=0, tiled=True)
    grad_input, grad_filter, grad_gate = to_rows(outs_rows)

    kept, up1, up2, up3 = grad_weight_part(after(at, skip_sum), ring, cot_all)
    moved = [shift(up1, "y", 1), shift(up2, "y", 2), shift(up3, "y", -1)]
    weight = weight_sum(at, [kept] + moved)
    return (grad_input, grad_gate, grad_filter, jnp.sum(skip_sum, axis=1), weight)


def solution(mesh):
    fine = Mesh(mesh.devices.reshape(NY, NZ, NX, NH), ("y", "z", "x", "core"))
    seq, ch = ("y", "z"), ("x", "core")
    rows = P(seq, ch)
    vector = P(ch + seq)
    weights = P(ch, seq)
    return jax.shard_map(
        ordered,
        mesh=fine,
        in_specs=(rows, rows, rows, vector, weights, rows),
        out_specs=(rows, rows, rows, vector, weights),
        check_vma=False,
    )
```

```python
import math

import jax
import jax.numpy as jnp
import numpy as np
from jax import lax
from jax.experimental import pallas as pl
from jax.experimental.pallas import tpu as pltpu
from jax.sharding import Mesh
from jax.sharding import PartitionSpec as P

NY, NZ, NX, NH = 4, 8, 4, 2
NS = NY * NZ
TOK = 128
CL = 32
CC = 16
FREQ = 2 * NS * TOK
ROOT = 1.0 / math.sqrt(NS * TOK)
bf16, f32 = jnp.bfloat16, jnp.float32


def halves(matrix):
    high = matrix.astype(jnp.bfloat16)
    low = (matrix - high.astype(np.float64)).astype(jnp.bfloat16)
    return high, low


def tables():
    k = np.arange(NS)[:, None] + 0.5
    n = np.arange(NS)[None, :]
    m = np.arange(TOK)[None, :]
    outer = 2.0 * np.pi * k * n / (2 * NS)
    a = np.concatenate([np.cos(outer), -np.sin(outer)], axis=0)
    a_inv = np.concatenate([np.cos(outer).T, -np.sin(outer).T], axis=1) * (2.0 / FREQ)
    turn = 2.0 * np.pi * k * m / FREQ
    inner = 2.0 * np.pi * (np.arange(TOK)[:, None] * m % TOK) / TOK
    c, s = np.cos(inner), np.sin(inner)
    b = np.block([[c, -s], [s, c]])
    b_inv = np.block([[c, s], [-s, c]])
    a_hi, a_lo = halves(a)
    i_hi, i_lo = halves(a_inv)
    b_hi, b_lo = halves(b)
    v_hi, v_lo = halves(b_inv)
    return (
        np.concatenate([a_hi, a_lo], axis=1),
        np.concatenate([i_hi, i_lo], axis=1),
        np.stack([b_hi, b_lo]),
        np.stack([v_hi, v_lo]),
        np.stack([np.cos(turn), np.sin(turn)]).astype(np.float32),
    )


def dot(x, y):
    return jnp.dot(x, y, preferred_element_type=f32)


def split(x):
    high = x.astype(bf16)
    return high, (x - high.astype(f32)).astype(bf16)


def rows_of(ref, c):
    return ref[pl.ds(c, NS, stride=CC), :]


def forward(src, a_ref, b_ref, t_ref):
    x = jnp.concatenate([rows_of(src, c) for c in range(CC)], axis=1).astype(bf16)
    a = a_ref[...]
    z = dot(a[:, :NS], x) + dot(a[:, NS:], x)
    tc, ts = t_ref[0], t_ref[1]
    parts = []
    for c in range(CC):
        re = z[:NS, c * TOK : (c + 1) * TOK]
        im = z[NS:, c * TOK : (c + 1) * TOK]
        parts.append(jnp.concatenate([re * tc + im * ts, im * tc - re * ts], axis=1))
    hi, lo = split(jnp.concatenate(parts, axis=0))
    return dot(hi, b_ref[0]) + dot(hi, b_ref[1]) + dot(lo, b_ref[0])


def inverse(spec, i_ref, v_ref, t_ref, dst):
    hi, lo = split(spec)
    v = dot(hi, v_ref[0]) + dot(hi, v_ref[1]) + dot(lo, v_ref[0])
    tc, ts = t_ref[0], t_ref[1]
    parts = []
    for c in range(CC):
        re = v[c * NS : (c + 1) * NS, :TOK]
        im = v[c * NS : (c + 1) * NS, TOK:]
        parts.append(jnp.concatenate([re * tc - im * ts, im * tc + re * ts], axis=0))
    hi, lo = split(jnp.concatenate(parts, axis=1))
    a = i_ref[...]
    y = dot(a[:, : 2 * NS], hi) + dot(a[:, 2 * NS :], hi) + dot(a[:, : 2 * NS], lo)
    for c in range(CC):
        dst[pl.ds(c, NS, stride=CC), :] = y[:, c * TOK : (c + 1) * TOK]


def times(p, q):
    pr, pi, qr, qi = p[:, :TOK], p[:, TOK:], q[:, :TOK], q[:, TOK:]
    return jnp.concatenate([pr * qr - pi * qi, pr * qi + pi * qr], axis=1)


def times_conj(p, q):
    pr, pi, qr, qi = p[:, :TOK], p[:, TOK:], q[:, :TOK], q[:, TOK:]
    return jnp.concatenate([pr * qr + pi * qi, pi * qr - pr * qi], axis=1)


def flat(x):
    return x.reshape(NS * CC, TOK)


def conv_kernel(in_ref, skip_ref, a_ref, i_ref, b_ref, v_ref, t_ref, mixed_ref, gated_ref, sig_ref, tap_ref, buf):
    buf[...] = flat(in_ref[:, 1].astype(f32))
    tap = forward(buf, a_ref, b_ref, t_ref)
    tap_ref[...] = tap
    buf[...] = flat(in_ref[:, 0].astype(f32))
    sig = forward(buf, a_ref, b_ref, t_ref)
    sig_ref[...] = sig
    inverse(times(sig, tap), i_ref, v_ref, t_ref, buf)
    skip = skip_ref[...]
    for n in range(NS):
        mixed = (buf[n * CC : (n + 1) * CC, :] + skip * in_ref[n, 0].astype(f32)).astype(bf16)
        mixed_ref[n] = mixed
        gated = in_ref[n, 2].astype(f32) * mixed.astype(f32)
        z = n % NZ
        gated_ref[n // NZ, :, z * TOK : (z + 1) * TOK] = gated.astype(bf16)


def back_kernel(gg_ref, in_ref, mixed_ref, sig_ref, tap_ref, skip_ref, a_ref, i_ref, b_ref, v_ref, t_ref, out_ref, gs_ref, buf, gmb):
    total = jnp.zeros((CC, TOK), f32)
    for n in range(NS):
        z = n % NZ
        gg = gg_ref[n // NZ, :, z * TOK : (z + 1) * TOK].astype(f32)
        out_ref[n, 2] = (gg * mixed_ref[n].astype(f32)).astype(bf16)
        gm = (gg * in_ref[n, 2].astype(f32)).astype(bf16).astype(f32)
        gmb[n * CC : (n + 1) * CC, :] = gm
        total = total + gm * in_ref[n, 0].astype(f32)
    gs_ref[...] = total * ROOT
    grad = forward(gmb, a_ref, b_ref, t_ref)
    inverse(times_conj(grad, tap_ref[...]), i_ref, v_ref, t_ref, buf)
    skip = skip_ref[...]
    for n in range(NS):
        rows = slice(n * CC, (n + 1) * CC)
        out_ref[n, 0] = (buf[rows, :] + skip * gmb[rows, :]).astype(bf16)
    inverse(times_conj(grad, sig_ref[...]), i_ref, v_ref, t_ref, buf)
    for n in range(NS):
        rows = slice(n * CC, (n + 1) * CC)
        out_ref[n, 1] = (buf[rows, :] * ROOT).astype(bf16)


def whole(array):
    rank = array.ndim
    return pl.BlockSpec(array.shape, lambda i: (0,) * rank)


STEPS = CL // CC
PACK = pl.BlockSpec((NS, 3, CC, TOK), lambda i: (0, 0, i, 0))
PLAIN = pl.BlockSpec((NS, CC, TOK), lambda i: (0, i, 0))
WIDE = pl.BlockSpec((NY, CC, NZ * TOK), lambda i: (0, i, 0))
SPEC = pl.BlockSpec((CC * NS, 2 * TOK), lambda i: (i, 0))
LANE = pl.BlockSpec((CC, TOK), lambda i: (i, 0))
SHAPE = jax.ShapeDtypeStruct


def conv(cols, skip, tabs):
    return pl.pallas_call(
        conv_kernel,
        grid=(STEPS,),
        in_specs=[PACK, LANE] + [whole(t) for t in tabs],
        out_specs=[PLAIN, WIDE, SPEC, SPEC],
        out_shape=[
            SHAPE((NS, CL, TOK), bf16),
            SHAPE((NY, CL, NZ * TOK), bf16),
            SHAPE((CL * NS, 2 * TOK), f32),
            SHAPE((CL * NS, 2 * TOK), f32),
        ],
        scratch_shapes=[pltpu.VMEM((NS * CC, TOK), f32)],
        name="conv",
    )(cols, skip, *tabs)


def back(gg, cols, mixed, sig, tap, skip, tabs):
    return pl.pallas_call(
        back_kernel,
        grid=(STEPS,),
        in_specs=[WIDE, PACK, PLAIN, SPEC, SPEC, LANE] + [whole(t) for t in tabs],
        out_specs=[PACK, LANE],
        out_shape=[SHAPE((NS, 3, CL, TOK), bf16), SHAPE((CL, TOK), f32)],
        scratch_shapes=[pltpu.VMEM((NS * CC, TOK), f32)] * 2,
        name="back",
    )(gg, cols, mixed, sig, tap, skip, *tabs)


def to_cols_kernel(s_ref, f_ref, g_ref, out_ref):
    for i, ref in enumerate((s_ref, f_ref, g_ref)):
        for b in range(ref.shape[1] // TOK):
            turned = ref[:, b * TOK : (b + 1) * TOK].T
            for j in range(TOK // CL):
                out_ref[b * (TOK // CL) + j, i] = turned[j * CL : (j + 1) * CL, :]


def to_cols(signal, taps, gate):
    width = signal.shape[1]
    span = 4 * TOK
    block = pl.BlockSpec((TOK, span), lambda i: (0, i))
    return pl.pallas_call(
        to_cols_kernel,
        grid=(width // span,),
        in_specs=[block] * 3,
        out_specs=pl.BlockSpec((span // CL, 3, CL, TOK), lambda i: (i, 0, 0, 0)),
        out_shape=SHAPE((NS, 3, CL, TOK), bf16),
        name="to_cols",
    )(signal, taps, gate)


def to_rows_kernel(in_ref, a_ref, b_ref, c_ref):
    for i, ref in enumerate((a_ref, b_ref, c_ref)):
        for b in range(ref.shape[1] // TOK):
            first = b * (TOK // CL)
            stacked = jnp.concatenate([in_ref[first + j, i] for j in range(TOK // CL)], axis=0)
            ref[:, b * TOK : (b + 1) * TOK] = stacked.T


def to_rows(cols):
    span = 4 * TOK
    block = pl.BlockSpec((TOK, span), lambda i: (0, i))
    out = SHAPE((TOK, NS * CL), bf16)
    return pl.pallas_call(
        to_rows_kernel,
        grid=(NS * CL // span,),
        in_specs=[pl.BlockSpec((span // CL, 3, CL, TOK), lambda i: (i, 0, 0, 0))],
        out_specs=[block] * 3,
        out_shape=[out] * 3,
        name="to_rows",
    )(cols)


OWN = (3, 2, 1, 6, 7, 0)
SENT = (4, 5)


def product(at, offsets, ws, cot_ref):
    y, z = at[0], at[1]
    total = None
    for r, w in enumerate(ws):
        rows = [
            w[pl.ds(pl.multiple_of((b * NZ + (z + offset) % NZ) * CL, CL), CL), :]
            for offset in offsets
            for b in range(NY)
        ]
        part = lax.dot_general(
            jnp.concatenate(rows, axis=0),
            cot_ref[(y + r) % NY],
            (((1,), (1,)), ((), ())),
            preferred_element_type=f32,
        )
        total = part if total is None else total + part
    return total


def opening_kernel(at, w0, w1, w2, w3, m0, m1, m2, m3, o0, o1, o2, o3, cot_ref, up_ref, down_ref):
    x, core = at[2], at[3]
    for s, (m, o) in enumerate(((m0, o0), (m1, o1), (m2, o2), (m3, o3))):
        mine, other = m[...], o[...]
        first = jnp.where(core == 0, mine, other)
        second = jnp.where(core == 0, other, mine)
        cot_ref[(x + s) % NX] = jnp.concatenate([first, second], axis=1)
    total = product(at, SENT, (w0, w1, w2, w3), cot_ref)
    up_ref[...] = total[: NY * CL].astype(bf16)
    down_ref[...] = total[NY * CL :].astype(bf16)


def opening_part(at, ws, mine, other):
    c, f = ws[0].shape
    t = mine[0].shape[0]
    span = 2 * TOK
    chain = pl.BlockSpec((NY * CL, span), lambda i, at: (0, i))
    return pl.pallas_call(
        opening_kernel,
        grid_spec=pltpu.PrefetchScalarGridSpec(
            num_scalar_prefetch=1,
            grid=(t // span,),
            in_specs=[pl.BlockSpec((c, f), lambda i, at: (0, 0))] * NY
            + [pl.BlockSpec((span, f // NH), lambda i, at: (i, 0))] * (2 * NX),
            out_specs=[pl.BlockSpec((NX, span, f), lambda i, at: (0, i, 0)), chain, chain],
        ),
        out_shape=[SHAPE((NX, t, f), bf16), SHAPE((NY * CL, t), bf16), SHAPE((NY * CL, t), bf16)],
        name="opening",
    )(at, *ws, *mine, *other)


def staying_kernel(at, w0, w1, w2, w3, cot_ref, own_ref):
    total = product(at, OWN, (w0, w1, w2, w3), cot_ref)
    for i in range(len(OWN)):
        own_ref[i] = total[i * NY * CL : (i + 1) * NY * CL]


def staying_part(at, ws, cot_all):
    c, f = ws[0].shape
    t = cot_all.shape[1]
    span = 2 * TOK
    return pl.pallas_call(
        staying_kernel,
        grid_spec=pltpu.PrefetchScalarGridSpec(
            num_scalar_prefetch=1,
            grid=(t // span,),
            in_specs=[pl.BlockSpec((c, f), lambda i, at: (0, 0))] * NY
            + [pl.BlockSpec((NX, span, f), lambda i, at: (0, i, 0))],
            out_specs=pl.BlockSpec((len(OWN), NY * CL, span), lambda i, at: (0, 0, i)),
        ),
        out_shape=SHAPE((len(OWN), NY * CL, t), f32),
        name="staying",
    )(at, *ws, cot_all)


def weight_kernel(at, *refs):
    pieces, cot_ref, outs, gated = refs[: NZ + 1], refs[NZ + 1], refs[NZ + 2 : -1], refs[-1]
    step = pl.program_id(0)

    @pl.when(step == 0)
    def _():
        row = 0
        for piece in pieces:
            gated[row : row + piece.shape[0], :] = piece[...]
            row += piece.shape[0]

    part = (dot(gated[...], cot_ref[0]) * ROOT).astype(bf16)
    for i, out in enumerate(outs):

        @pl.when(step == i)
        def _():
            out[...] = part


def grad_weight_part(at, pieces, cot_all):
    c, t, f = NS * CL, cot_all.shape[1], cot_all.shape[2]
    return pl.pallas_call(
        weight_kernel,
        grid_spec=pltpu.PrefetchScalarGridSpec(
            num_scalar_prefetch=1,
            grid=(NY,),
            in_specs=[pl.BlockSpec(p.shape, lambda i, at: (0, 0)) for p in pieces]
            + [pl.BlockSpec((1, t, f), lambda i, at: ((at[0] + i) % NY, 0, 0))],
            out_specs=[pl.BlockSpec((c, f), lambda i, at: (0, 0))] * NY,
            scratch_shapes=[pltpu.VMEM((c, t), bf16)],
        ),
        out_shape=[SHAPE((c, f), bf16)] * NY,
        name="grad_weight",
    )(at, *pieces, cot_all)


def sum_kernel(at, a_ref, b_ref, c_ref, d_ref, out_ref):
    z = at[1]
    for r in range(NZ):
        for b in range(NY):
            rows = slice((r * NY + b) * CL, (r * NY + b + 1) * CL)
            total = a_ref[rows, :].astype(f32) + b_ref[rows, :].astype(f32)
            total = total + c_ref[rows, :].astype(f32) + d_ref[rows, :].astype(f32)
            out_ref[b, (z + r) % NZ] = total


def weight_sum(at, parts):
    c, f = parts[0].shape
    return pl.pallas_call(
        sum_kernel,
        grid_spec=pltpu.PrefetchScalarGridSpec(
            num_scalar_prefetch=1,
            grid=(f // TOK,),
            in_specs=[pl.BlockSpec((c, TOK), lambda i, at: (0, i))] * NY,
            out_specs=pl.BlockSpec((NY, NZ, CL, TOK), lambda i, at: (0, 0, 0, i)),
        ),
        out_shape=SHAPE((NY, NZ, CL, f), f32),
        name="weight_sum",
    )(at, *parts).reshape(c, f)


def shift(value, axis, by):
    count = lax.axis_size(axis)
    return lax.ppermute(value, axis, [(i, (i + by) % count) for i in range(count)])


def add(received, own):
    return (received.astype(f32) + own).astype(bf16)


def after(value, *earlier):
    return lax.optimization_barrier((value,) + earlier)[0]


def ordered(signal, gate_values, filter_taps, skip_gain, w_out, cotangent):
    tabs = [jnp.asarray(t) for t in tables()]
    seq = ("y", "z")
    at = jnp.stack([lax.axis_index(a) for a in ("y", "z", "x", "core")]).astype(jnp.int32)

    pieces = cotangent.reshape(TOK, NZ // NH, NH, TOK).transpose(2, 1, 0, 3)
    pieces = lax.all_to_all(pieces, "core", split_axis=0, concat_axis=0, tiled=True)
    piece = lax.all_to_all(pieces.reshape(NZ, TOK, TOK), "z", split_axis=0, concat_axis=0, tiled=True)
    piece = piece.reshape(NZ * TOK, TOK)

    cols = to_cols(after(signal, pieces), filter_taps, gate_values)
    cols = lax.all_to_all(cols, seq, split_axis=0, concat_axis=0, tiled=True)
    ws = [w_out, shift(w_out, "y", -1), shift(w_out, "y", 2), shift(w_out, "y", 1)]
    skip = jnp.broadcast_to(skip_gain[:, None], (CL, TOK))

    other = shift(piece, "core", 1)
    mine = [piece, shift(piece, "x", -1), shift(piece, "x", 2), shift(piece, "x", 1)]
    mixed, gated, sig_spec, tap_spec = conv(cols, skip, tabs)
    gated = lax.all_to_all(gated, "y", split_axis=0, concat_axis=0, tiled=True)
    gated = gated.reshape(NY * CL, NZ * TOK)
    other = [other] + [shift(m, "core", 1) for m in mine[1:]]

    cot_all, up, down = opening_part(at, ws, mine, other)
    up = shift(up, "z", 1)
    down = shift(down, "z", -1)
    own = staying_part(at, ws, cot_all)

    for i in range(2):
        up, down = lax.optimization_barrier((up, down))
        up, down = add(up, own[i]), add(down, own[3 + i])
        up = shift(up, "z", 1)
        down = shift(down, "z", -1)
    up, down = lax.optimization_barrier((up, down))
    rest = down.astype(f32) + own[5]
    up = shift(add(up, own[2]), "z", 1)
    part = (up.astype(f32) + rest).astype(bf16)

    fore, aft = [gated], [gated]
    for _ in range(3):
        fore.append(shift(fore[-1], "z", 1))
        aft.append(shift(aft[-1], "z", -1))
    half = NY * CL // 2
    far = [shift(fore[-1][:half], "z", 1), shift(aft[-1][half:], "z", -1)]
    ring = [gated] + aft[1:] + far + fore[:0:-1]

    part = part.reshape(NY, CL, NZ * TOK)
    grad_gated = lax.all_to_all(part, "y", split_axis=0, concat_axis=0, tiled=True)
    outs, skip_sum = back(grad_gated, cols, mixed, sig_spec, tap_spec, skip, tabs)
    outs_rows = lax.all_to_all(outs, seq, split_axis=0, concat_axis=0, tiled=True)
    kept, up1, up2, up3 = grad_weight_part(at, ring, cot_all)
    moved = [shift(up1, "y", 1), shift(up2, "y", 2), shift(up3, "y", -1)]
    weight = weight_sum(at, [kept] + moved)
    grad_input, grad_filter, grad_gate = to_rows(outs_rows)
    return (grad_input, grad_gate, grad_filter, jnp.sum(skip_sum, axis=1), weight)


def solution(mesh):
    fine = Mesh(mesh.devices.reshape(NY, NZ, NX, NH), ("y", "z", "x", "core"))
    seq, ch = ("y", "z"), ("x", "core")
    rows = P(seq, ch)
    vector = P(ch + seq)
    weights = P(ch, seq)
    return jax.shard_map(
        ordered,
        mesh=fine,
        in_specs=(rows, rows, rows, vector, weights, rows),
        out_specs=(rows, rows, rows, vector, weights),
        check_vma=False,
    )
```

```python
import math

import jax
import jax.numpy as jnp
import numpy as np
from jax import lax
from jax.experimental import pallas as pl
from jax.experimental.pallas import tpu as pltpu
from jax.sharding import Mesh
from jax.sharding import PartitionSpec as P

NY, NZ, NX, NH = 4, 8, 4, 2
NS = NY * NZ
TOK = 128
CL = 32
CC = 16
FREQ = 2 * NS * TOK
ROOT = 1.0 / math.sqrt(NS * TOK)
bf16, f32 = jnp.bfloat16, jnp.float32


def halves(matrix):
    high = matrix.astype(jnp.bfloat16)
    low = (matrix - high.astype(np.float64)).astype(jnp.bfloat16)
    return high, low


def tables():
    k = np.arange(NS)[:, None] + 0.5
    n = np.arange(NS)[None, :]
    m = np.arange(TOK)[None, :]
    outer = 2.0 * np.pi * k * n / (2 * NS)
    a = np.concatenate([np.cos(outer), -np.sin(outer)], axis=0)
    a_inv = np.concatenate([np.cos(outer).T, -np.sin(outer).T], axis=1) * (2.0 / FREQ)
    turn = 2.0 * np.pi * k * m / FREQ
    inner = 2.0 * np.pi * (np.arange(TOK)[:, None] * m % TOK) / TOK
    c, s = np.cos(inner), np.sin(inner)
    b = np.block([[c, -s], [s, c]])
    b_inv = np.block([[c, s], [-s, c]])
    a_hi, a_lo = halves(a)
    i_hi, i_lo = halves(a_inv)
    b_hi, b_lo = halves(b)
    v_hi, v_lo = halves(b_inv)
    return (
        np.concatenate([a_hi, a_lo], axis=1),
        np.concatenate([i_hi, i_lo], axis=1),
        np.stack([b_hi, b_lo]),
        np.stack([v_hi, v_lo]),
        np.stack([np.cos(turn), np.sin(turn)]).astype(np.float32),
    )


def dot(x, y):
    return jnp.dot(x, y, preferred_element_type=f32)


def split(x):
    high = x.astype(bf16)
    return high, (x - high.astype(f32)).astype(bf16)


def rows_of(ref, c):
    return ref[pl.ds(c, NS, stride=CC), :]


def forward(src, a_ref, b_ref, t_ref):
    x = jnp.concatenate([rows_of(src, c) for c in range(CC)], axis=1).astype(bf16)
    a = a_ref[...]
    z = dot(a[:, :NS], x) + dot(a[:, NS:], x)
    tc, ts = t_ref[0], t_ref[1]
    parts = []
    for c in range(CC):
        re = z[:NS, c * TOK : (c + 1) * TOK]
        im = z[NS:, c * TOK : (c + 1) * TOK]
        parts.append(jnp.concatenate([re * tc + im * ts, im * tc - re * ts], axis=1))
    hi, lo = split(jnp.concatenate(parts, axis=0))
    return dot(hi, b_ref[0]) + dot(hi, b_ref[1]) + dot(lo, b_ref[0])


def inverse(spec, i_ref, v_ref, t_ref, dst):
    hi, lo = split(spec)
    v = dot(hi, v_ref[0]) + dot(hi, v_ref[1]) + dot(lo, v_ref[0])
    tc, ts = t_ref[0], t_ref[1]
    parts = []
    for c in range(CC):
        re = v[c * NS : (c + 1) * NS, :TOK]
        im = v[c * NS : (c + 1) * NS, TOK:]
        parts.append(jnp.concatenate([re * tc - im * ts, im * tc + re * ts], axis=0))
    hi, lo = split(jnp.concatenate(parts, axis=1))
    a = i_ref[...]
    y = dot(a[:, : 2 * NS], hi) + dot(a[:, 2 * NS :], hi) + dot(a[:, : 2 * NS], lo)
    for c in range(CC):
        dst[pl.ds(c, NS, stride=CC), :] = y[:, c * TOK : (c + 1) * TOK]


def times(p, q):
    pr, pi, qr, qi = p[:, :TOK], p[:, TOK:], q[:, :TOK], q[:, TOK:]
    return jnp.concatenate([pr * qr - pi * qi, pr * qi + pi * qr], axis=1)


def times_conj(p, q):
    pr, pi, qr, qi = p[:, :TOK], p[:, TOK:], q[:, :TOK], q[:, TOK:]
    return jnp.concatenate([pr * qr + pi * qi, pi * qr - pr * qi], axis=1)


def flat(x):
    return x.reshape(NS * CC, TOK)


def conv_kernel(in_ref, skip_ref, a_ref, i_ref, b_ref, v_ref, t_ref, mixed_ref, gated_ref, sig_ref, tap_ref, buf):
    buf[...] = flat(in_ref[:, 1].astype(f32))
    tap = forward(buf, a_ref, b_ref, t_ref)
    tap_ref[...] = tap
    buf[...] = flat(in_ref[:, 0].astype(f32))
    sig = forward(buf, a_ref, b_ref, t_ref)
    sig_ref[...] = sig
    inverse(times(sig, tap), i_ref, v_ref, t_ref, buf)
    skip = skip_ref[...]
    for n in range(NS):
        mixed = (buf[n * CC : (n + 1) * CC, :] + skip * in_ref[n, 0].astype(f32)).astype(bf16)
        mixed_ref[n] = mixed
        gated = in_ref[n, 2].astype(f32) * mixed.astype(f32)
        z = n % NZ
        gated_ref[n // NZ, :, z * TOK : (z + 1) * TOK] = gated.astype(bf16)


def back_kernel(gg_ref, in_ref, mixed_ref, sig_ref, tap_ref, skip_ref, a_ref, i_ref, b_ref, v_ref, t_ref, out_ref, gs_ref, buf, gmb):
    total = jnp.zeros((CC, TOK), f32)
    for n in range(NS):
        z = n % NZ
        gg = gg_ref[n // NZ, :, z * TOK : (z + 1) * TOK].astype(f32)
        out_ref[n, 2] = (gg * mixed_ref[n].astype(f32)).astype(bf16)
        gm = (gg * in_ref[n, 2].astype(f32)).astype(bf16).astype(f32)
        gmb[n * CC : (n + 1) * CC, :] = gm
        total = total + gm * in_ref[n, 0].astype(f32)
    gs_ref[...] = total * ROOT
    grad = forward(gmb, a_ref, b_ref, t_ref)
    inverse(times_conj(grad, tap_ref[...]), i_ref, v_ref, t_ref, buf)
    skip = skip_ref[...]
    for n in range(NS):
        rows = slice(n * CC, (n + 1) * CC)
        out_ref[n, 0] = (buf[rows, :] + skip * gmb[rows, :]).astype(bf16)
    inverse(times_conj(grad, sig_ref[...]), i_ref, v_ref, t_ref, buf)
    for n in range(NS):
        rows = slice(n * CC, (n + 1) * CC)
        out_ref[n, 1] = (buf[rows, :] * ROOT).astype(bf16)


def whole(array):
    rank = array.ndim
    return pl.BlockSpec(array.shape, lambda i: (0,) * rank)


STEPS = CL // CC
PACK = pl.BlockSpec((NS, 3, CC, TOK), lambda i: (0, 0, i, 0))
PLAIN = pl.BlockSpec((NS, CC, TOK), lambda i: (0, i, 0))
WIDE = pl.BlockSpec((NY, CC, NZ * TOK), lambda i: (0, i, 0))
SPEC = pl.BlockSpec((CC * NS, 2 * TOK), lambda i: (i, 0))
LANE = pl.BlockSpec((CC, TOK), lambda i: (i, 0))
SHAPE = jax.ShapeDtypeStruct


def conv(cols, skip, tabs):
    return pl.pallas_call(
        conv_kernel,
        grid=(STEPS,),
        in_specs=[PACK, LANE] + [whole(t) for t in tabs],
        out_specs=[PLAIN, WIDE, SPEC, SPEC],
        out_shape=[
            SHAPE((NS, CL, TOK), bf16),
            SHAPE((NY, CL, NZ * TOK), bf16),
            SHAPE((CL * NS, 2 * TOK), f32),
            SHAPE((CL * NS, 2 * TOK), f32),
        ],
        scratch_shapes=[pltpu.VMEM((NS * CC, TOK), f32)],
        name="conv",
    )(cols, skip, *tabs)


def back(gg, cols, mixed, sig, tap, skip, tabs):
    return pl.pallas_call(
        back_kernel,
        grid=(STEPS,),
        in_specs=[WIDE, PACK, PLAIN, SPEC, SPEC, LANE] + [whole(t) for t in tabs],
        out_specs=[PACK, LANE],
        out_shape=[SHAPE((NS, 3, CL, TOK), bf16), SHAPE((CL, TOK), f32)],
        scratch_shapes=[pltpu.VMEM((NS * CC, TOK), f32)] * 2,
        name="back",
    )(gg, cols, mixed, sig, tap, skip, *tabs)


def to_cols_kernel(s_ref, f_ref, g_ref, out_ref):
    for i, ref in enumerate((s_ref, f_ref, g_ref)):
        for b in range(ref.shape[1] // TOK):
            turned = ref[:, b * TOK : (b + 1) * TOK].T
            for j in range(TOK // CL):
                out_ref[b * (TOK // CL) + j, i] = turned[j * CL : (j + 1) * CL, :]


def to_cols(signal, taps, gate):
    width = signal.shape[1]
    span = 4 * TOK
    block = pl.BlockSpec((TOK, span), lambda i: (0, i))
    return pl.pallas_call(
        to_cols_kernel,
        grid=(width // span,),
        in_specs=[block] * 3,
        out_specs=pl.BlockSpec((span // CL, 3, CL, TOK), lambda i: (i, 0, 0, 0)),
        out_shape=SHAPE((NS, 3, CL, TOK), bf16),
        name="to_cols",
    )(signal, taps, gate)


def to_rows_kernel(in_ref, a_ref, b_ref, c_ref):
    for i, ref in enumerate((a_ref, b_ref, c_ref)):
        for b in range(ref.shape[1] // TOK):
            first = b * (TOK // CL)
            stacked = jnp.concatenate([in_ref[first + j, i] for j in range(TOK // CL)], axis=0)
            ref[:, b * TOK : (b + 1) * TOK] = stacked.T


def to_rows(cols):
    span = 4 * TOK
    block = pl.BlockSpec((TOK, span), lambda i: (0, i))
    out = SHAPE((TOK, NS * CL), bf16)
    return pl.pallas_call(
        to_rows_kernel,
        grid=(NS * CL // span,),
        in_specs=[pl.BlockSpec((span // CL, 3, CL, TOK), lambda i: (i, 0, 0, 0))],
        out_specs=[block] * 3,
        out_shape=[out] * 3,
        name="to_rows",
    )(cols)


OWN = (3, 2, 1, 6, 7, 0)
SENT = (4, 5)


def product(at, offsets, ws, cot_ref):
    y, z = at[0], at[1]
    total = None
    for r, w in enumerate(ws):
        rows = [
            w[pl.ds(pl.multiple_of((b * NZ + (z + offset) % NZ) * CL, CL), CL), :]
            for offset in offsets
            for b in range(NY)
        ]
        part = lax.dot_general(
            jnp.concatenate(rows, axis=0),
            cot_ref[(y + r) % NY],
            (((1,), (1,)), ((), ())),
            preferred_element_type=f32,
        )
        total = part if total is None else total + part
    return total


def opening_kernel(at, w0, w1, w2, w3, m0, m1, m2, m3, o0, o1, o2, o3, cot_ref, up_ref, down_ref):
    x, core = at[2], at[3]
    for s, (m, o) in enumerate(((m0, o0), (m1, o1), (m2, o2), (m3, o3))):
        mine, other = m[...], o[...]
        first = jnp.where(core == 0, mine, other)
        second = jnp.where(core == 0, other, mine)
        cot_ref[(x + s) % NX] = jnp.concatenate([first, second], axis=1)
    total = product(at, SENT, (w0, w1, w2, w3), cot_ref)
    up_ref[...] = total[: NY * CL].astype(bf16)
    down_ref[...] = total[NY * CL :].astype(bf16)


def opening_part(at, ws, mine, other):
    c, f = ws[0].shape
    t = mine[0].shape[0]
    span = 2 * TOK
    chain = pl.BlockSpec((NY * CL, span), lambda i, at: (0, i))
    return pl.pallas_call(
        opening_kernel,
        grid_spec=pltpu.PrefetchScalarGridSpec(
            num_scalar_prefetch=1,
            grid=(t // span,),
            in_specs=[pl.BlockSpec((c, f), lambda i, at: (0, 0))] * NY
            + [pl.BlockSpec((span, f // NH), lambda i, at: (i, 0))] * (2 * NX),
            out_specs=[pl.BlockSpec((NX, span, f), lambda i, at: (0, i, 0)), chain, chain],
        ),
        out_shape=[SHAPE((NX, t, f), bf16), SHAPE((NY * CL, t), bf16), SHAPE((NY * CL, t), bf16)],
        name="opening",
    )(at, *ws, *mine, *other)


def staying_kernel(at, w0, w1, w2, w3, cot_ref, own_ref):
    total = product(at, OWN, (w0, w1, w2, w3), cot_ref)
    for i in range(len(OWN)):
        own_ref[i] = total[i * NY * CL : (i + 1) * NY * CL]


def staying_part(at, ws, cot_all):
    c, f = ws[0].shape
    t = cot_all.shape[1]
    span = 2 * TOK
    return pl.pallas_call(
        staying_kernel,
        grid_spec=pltpu.PrefetchScalarGridSpec(
            num_scalar_prefetch=1,
            grid=(t // span,),
            in_specs=[pl.BlockSpec((c, f), lambda i, at: (0, 0))] * NY
            + [pl.BlockSpec((NX, span, f), lambda i, at: (0, i, 0))],
            out_specs=pl.BlockSpec((len(OWN), NY * CL, span), lambda i, at: (0, 0, i)),
        ),
        out_shape=SHAPE((len(OWN), NY * CL, t), f32),
        name="staying",
    )(at, *ws, cot_all)


def weight_kernel(at, *refs):
    pieces, cot_ref, outs, gated = refs[:NZ], refs[NZ], refs[NZ + 1 : -1], refs[-1]
    step = pl.program_id(0)

    @pl.when(step == 0)
    def _():
        row = 0
        for piece in pieces:
            gated[row : row + piece.shape[0], :] = piece[...]
            row += piece.shape[0]

    part = (dot(gated[...], cot_ref[0]) * ROOT).astype(bf16)
    for i, out in enumerate(outs):

        @pl.when(step == i)
        def _():
            out[...] = part


def grad_weight_part(at, pieces, cot_all):
    c, t, f = NS * CL, cot_all.shape[1], cot_all.shape[2]
    return pl.pallas_call(
        weight_kernel,
        grid_spec=pltpu.PrefetchScalarGridSpec(
            num_scalar_prefetch=1,
            grid=(NY,),
            in_specs=[pl.BlockSpec(p.shape, lambda i, at: (0, 0)) for p in pieces]
            + [pl.BlockSpec((1, t, f), lambda i, at: ((at[0] + i) % NY, 0, 0))],
            out_specs=[pl.BlockSpec((c, f), lambda i, at: (0, 0))] * NY,
            scratch_shapes=[pltpu.VMEM((c, t), bf16)],
        ),
        out_shape=[SHAPE((c, f), bf16)] * NY,
        name="grad_weight",
    )(at, *pieces, cot_all)


def sum_kernel(at, a_ref, b_ref, c_ref, d_ref, out_ref):
    z = at[1]
    for r in range(NZ):
        for b in range(NY):
            rows = slice((r * NY + b) * CL, (r * NY + b + 1) * CL)
            total = a_ref[rows, :].astype(f32) + b_ref[rows, :].astype(f32)
            total = total + c_ref[rows, :].astype(f32) + d_ref[rows, :].astype(f32)
            out_ref[b, (z + r) % NZ] = total


def weight_sum(at, parts):
    c, f = parts[0].shape
    return pl.pallas_call(
        sum_kernel,
        grid_spec=pltpu.PrefetchScalarGridSpec(
            num_scalar_prefetch=1,
            grid=(f // TOK,),
            in_specs=[pl.BlockSpec((c, TOK), lambda i, at: (0, i))] * NY,
            out_specs=pl.BlockSpec((NY, NZ, CL, TOK), lambda i, at: (0, 0, 0, i)),
        ),
        out_shape=SHAPE((NY, NZ, CL, f), f32),
        name="weight_sum",
    )(at, *parts).reshape(c, f)


def cut_kernel(at, *refs):
    for i in range(NZ):
        refs[NZ + i][...] = refs[i][...]


def cut(at, cotangent):
    block = SHAPE((TOK, TOK), bf16)
    return pl.pallas_call(
        cut_kernel,
        grid_spec=pltpu.PrefetchScalarGridSpec(
            num_scalar_prefetch=1,
            grid=(1,),
            in_specs=[
                pl.BlockSpec((TOK, TOK), lambda i, at, r=r: (0, (at[1] + r) % NZ)) for r in range(NZ)
            ],
            out_specs=[pl.BlockSpec((TOK, TOK), lambda i, at: (0, 0))] * NZ,
        ),
        out_shape=[block] * NZ,
        name="cut",
    )(at, *[cotangent] * NZ)


def join_kernel(at, *refs):
    want = (at[1] % (NZ // NH)) * NH + at[3]
    for r in range(NZ):
        refs[NZ][(want - r + NZ) % NZ] = refs[r][...]


def join(at, moved):
    return pl.pallas_call(
        join_kernel,
        grid_spec=pltpu.PrefetchScalarGridSpec(
            num_scalar_prefetch=1,
            grid=(1,),
            in_specs=[pl.BlockSpec((TOK, TOK), lambda i, at: (0, 0))] * NZ,
            out_specs=pl.BlockSpec((NZ, TOK, TOK), lambda i, at: (0, 0, 0)),
        ),
        out_shape=SHAPE((NZ, TOK, TOK), bf16),
        name="join",
    )(at, *moved).reshape(NZ * TOK, TOK)


def spread(r):
    pairs = []
    for z in range(NZ):
        for core in range(NH):
            q = (z + r) % NZ
            pairs.append((z * NH + core, (NZ // NH * core + q // NH) * NH + q % NH))
    return pairs


def shift(value, axis, by):
    count = lax.axis_size(axis)
    return lax.ppermute(value, axis, [(i, (i + by) % count) for i in range(count)])


def add(received, own):
    return (received.astype(f32) + own).astype(bf16)


def ordered(signal, gate_values, filter_taps, skip_gain, w_out, cotangent):
    tabs = [jnp.asarray(t) for t in tables()]
    seq = ("y", "z")
    at = jnp.stack([lax.axis_index(a) for a in ("y", "z", "x", "core")]).astype(jnp.int32)

    cols = to_cols(signal, filter_taps, gate_values)
    cols = lax.all_to_all(cols, seq, split_axis=0, concat_axis=0, tiled=True)
    pieces = cut(at, cotangent)
    pieces = [lax.ppermute(p, ("z", "core"), spread(r)) for r, p in enumerate(pieces)]
    piece = join(at, pieces)
    ws = [w_out, shift(w_out, "y", -1), shift(w_out, "y", 2), shift(w_out, "y", 1)]
    skip = jnp.broadcast_to(skip_gain[:, None], (CL, TOK))

    other = shift(piece, "core", 1)
    mine = [piece, shift(piece, "x", -1), shift(piece, "x", 2), shift(piece, "x", 1)]
    mixed, gated, sig_spec, tap_spec = conv(cols, skip, tabs)
    gated = lax.all_to_all(gated, "y", split_axis=0, concat_axis=0, tiled=True)
    gated = gated.reshape(NY * CL, NZ * TOK)
    other = [other] + [shift(m, "core", 1) for m in mine[1:]]

    cot_all, up, down = opening_part(at, ws, mine, other)
    up = shift(up, "z", 1)
    down = shift(down, "z", -1)
    own = staying_part(at, ws, cot_all)

    for i in range(2):
        up, down = lax.optimization_barrier((up, down))
        up, down = add(up, own[i]), add(down, own[3 + i])
        up = shift(up, "z", 1)
        down = shift(down, "z", -1)
    up, down = lax.optimization_barrier((up, down))
    rest = down.astype(f32) + own[5]
    up = shift(add(up, own[2]), "z", 1)
    part = (up.astype(f32) + rest).astype(bf16)

    fore, aft = [gated], [gated]
    for _ in range(3):
        fore.append(shift(fore[-1], "z", 1))
        aft.append(shift(aft[-1], "z", -1))
    far = shift(fore[-1], "z", 1)
    ring = [gated] + aft[1:] + [far] + fore[:0:-1]

    part = part.reshape(NY, CL, NZ * TOK)
    grad_gated = lax.all_to_all(part, "y", split_axis=0, concat_axis=0, tiled=True)
    outs, skip_sum = back(grad_gated, cols, mixed, sig_spec, tap_spec, skip, tabs)
    outs_rows = lax.all_to_all(outs, seq, split_axis=0, concat_axis=0, tiled=True)
    kept, up1, up2, up3 = grad_weight_part(at, ring, cot_all)
    moved = [shift(up1, "y", 1), shift(up2, "y", 2), shift(up3, "y", -1)]
    weight = weight_sum(at, [kept] + moved)
    grad_input, grad_filter, grad_gate = to_rows(outs_rows)
    return (grad_input, grad_gate, grad_filter, jnp.sum(skip_sum, axis=1), weight)


def solution(mesh):
    fine = Mesh(mesh.devices.reshape(NY, NZ, NX, NH), ("y", "z", "x", "core"))
    seq, ch = ("y", "z"), ("x", "core")
    rows = P(seq, ch)
    vector = P(ch + seq)
    weights = P(ch, seq)
    return jax.shard_map(
        ordered,
        mesh=fine,
        in_specs=(rows, rows, rows, vector, weights, rows),
        out_specs=(rows, rows, rows, vector, weights),
        check_vma=False,
    )
```

```python
import math

import jax
import jax.numpy as jnp
import numpy as np
from jax import lax
from jax.experimental import pallas as pl
from jax.experimental.pallas import tpu as pltpu
from jax.sharding import Mesh
from jax.sharding import PartitionSpec as P

NY, NZ, NX, NH = 4, 8, 4, 2
NS = NY * NZ
TOK = 128
CL = 32
CC = 16
FREQ = 2 * NS * TOK
ROOT = 1.0 / math.sqrt(NS * TOK)
bf16, f32 = jnp.bfloat16, jnp.float32


def halves(matrix):
    high = matrix.astype(jnp.bfloat16)
    low = (matrix - high.astype(np.float64)).astype(jnp.bfloat16)
    return high, low


def tables():
    k = np.arange(NS)[:, None] + 0.5
    n = np.arange(NS)[None, :]
    m = np.arange(TOK)[None, :]
    outer = 2.0 * np.pi * k * n / (2 * NS)
    a = np.concatenate([np.cos(outer), -np.sin(outer)], axis=0)
    a_inv = np.concatenate([np.cos(outer).T, -np.sin(outer).T], axis=1) * (2.0 / FREQ)
    turn = 2.0 * np.pi * k * m / FREQ
    inner = 2.0 * np.pi * (np.arange(TOK)[:, None] * m % TOK) / TOK
    c, s = np.cos(inner), np.sin(inner)
    b = np.block([[c, -s], [s, c]])
    b_inv = np.block([[c, s], [-s, c]])
    a_hi, a_lo = halves(a)
    i_hi, i_lo = halves(a_inv)
    b_hi, b_lo = halves(b)
    v_hi, v_lo = halves(b_inv)
    return (
        np.concatenate([a_hi, a_lo], axis=1),
        np.concatenate([i_hi, i_lo], axis=1),
        np.stack([b_hi, b_lo]),
        np.stack([v_hi, v_lo]),
        np.stack([np.cos(turn), np.sin(turn)]).astype(np.float32),
    )


def dot(x, y):
    return jnp.dot(x, y, preferred_element_type=f32)


def split(x):
    high = x.astype(bf16)
    return high, (x - high.astype(f32)).astype(bf16)


def rows_of(ref, c):
    return ref[pl.ds(c, NS, stride=CC), :]


def forward(src, a_ref, b_ref, t_ref):
    x = jnp.concatenate([rows_of(src, c) for c in range(CC)], axis=1).astype(bf16)
    a = a_ref[...]
    z = dot(a[:, :NS], x) + dot(a[:, NS:], x)
    tc, ts = t_ref[0], t_ref[1]
    parts = []
    for c in range(CC):
        re = z[:NS, c * TOK : (c + 1) * TOK]
        im = z[NS:, c * TOK : (c + 1) * TOK]
        parts.append(jnp.concatenate([re * tc + im * ts, im * tc - re * ts], axis=1))
    hi, lo = split(jnp.concatenate(parts, axis=0))
    return dot(hi, b_ref[0]) + dot(hi, b_ref[1]) + dot(lo, b_ref[0])


def inverse(spec, i_ref, v_ref, t_ref, dst):
    hi, lo = split(spec)
    v = dot(hi, v_ref[0]) + dot(hi, v_ref[1]) + dot(lo, v_ref[0])
    tc, ts = t_ref[0], t_ref[1]
    parts = []
    for c in range(CC):
        re = v[c * NS : (c + 1) * NS, :TOK]
        im = v[c * NS : (c + 1) * NS, TOK:]
        parts.append(jnp.concatenate([re * tc - im * ts, im * tc + re * ts], axis=0))
    hi, lo = split(jnp.concatenate(parts, axis=1))
    a = i_ref[...]
    y = dot(a[:, : 2 * NS], hi) + dot(a[:, 2 * NS :], hi) + dot(a[:, : 2 * NS], lo)
    for c in range(CC):
        dst[pl.ds(c, NS, stride=CC), :] = y[:, c * TOK : (c + 1) * TOK]


def times(p, q):
    pr, pi, qr, qi = p[:, :TOK], p[:, TOK:], q[:, :TOK], q[:, TOK:]
    return jnp.concatenate([pr * qr - pi * qi, pr * qi + pi * qr], axis=1)


def times_conj(p, q):
    pr, pi, qr, qi = p[:, :TOK], p[:, TOK:], q[:, :TOK], q[:, TOK:]
    return jnp.concatenate([pr * qr + pi * qi, pi * qr - pr * qi], axis=1)


def flat(x):
    return x.reshape(NS * CC, TOK)


def conv_kernel(in_ref, skip_ref, a_ref, i_ref, b_ref, v_ref, t_ref, mixed_ref, gated_ref, sig_ref, tap_ref, buf):
    buf[...] = flat(in_ref[:, 1].astype(f32))
    tap = forward(buf, a_ref, b_ref, t_ref)
    tap_ref[...] = tap
    buf[...] = flat(in_ref[:, 0].astype(f32))
    sig = forward(buf, a_ref, b_ref, t_ref)
    sig_ref[...] = sig
    inverse(times(sig, tap), i_ref, v_ref, t_ref, buf)
    skip = skip_ref[...]
    for n in range(NS):
        mixed = (buf[n * CC : (n + 1) * CC, :] + skip * in_ref[n, 0].astype(f32)).astype(bf16)
        mixed_ref[n] = mixed
        gated = in_ref[n, 2].astype(f32) * mixed.astype(f32)
        z = n % NZ
        gated_ref[n // NZ, :, z * TOK : (z + 1) * TOK] = gated.astype(bf16)


def back_kernel(gg_ref, in_ref, mixed_ref, sig_ref, tap_ref, skip_ref, a_ref, i_ref, b_ref, v_ref, t_ref, out_ref, gs_ref, buf, gmb):
    total = jnp.zeros((CC, TOK), f32)
    for n in range(NS):
        z = n % NZ
        gg = gg_ref[n // NZ, :, z * TOK : (z + 1) * TOK].astype(f32)
        out_ref[n, 2] = (gg * mixed_ref[n].astype(f32)).astype(bf16)
        gm = (gg * in_ref[n, 2].astype(f32)).astype(bf16).astype(f32)
        gmb[n * CC : (n + 1) * CC, :] = gm
        total = total + gm * in_ref[n, 0].astype(f32)
    gs_ref[...] = total * ROOT
    grad = forward(gmb, a_ref, b_ref, t_ref)
    inverse(times_conj(grad, tap_ref[...]), i_ref, v_ref, t_ref, buf)
    skip = skip_ref[...]
    for n in range(NS):
        rows = slice(n * CC, (n + 1) * CC)
        out_ref[n, 0] = (buf[rows, :] + skip * gmb[rows, :]).astype(bf16)
    inverse(times_conj(grad, sig_ref[...]), i_ref, v_ref, t_ref, buf)
    for n in range(NS):
        rows = slice(n * CC, (n + 1) * CC)
        out_ref[n, 1] = (buf[rows, :] * ROOT).astype(bf16)


def whole(array):
    rank = array.ndim
    return pl.BlockSpec(array.shape, lambda i: (0,) * rank)


STEPS = CL // CC
PACK = pl.BlockSpec((NS, 3, CC, TOK), lambda i: (0, 0, i, 0))
PLAIN = pl.BlockSpec((NS, CC, TOK), lambda i: (0, i, 0))
WIDE = pl.BlockSpec((NY, CC, NZ * TOK), lambda i: (0, i, 0))
SPEC = pl.BlockSpec((CC * NS, 2 * TOK), lambda i: (i, 0))
LANE = pl.BlockSpec((CC, TOK), lambda i: (i, 0))
SHAPE = jax.ShapeDtypeStruct


def conv(cols, skip, tabs):
    return pl.pallas_call(
        conv_kernel,
        grid=(STEPS,),
        in_specs=[PACK, LANE] + [whole(t) for t in tabs],
        out_specs=[PLAIN, WIDE, SPEC, SPEC],
        out_shape=[
            SHAPE((NS, CL, TOK), bf16),
            SHAPE((NY, CL, NZ * TOK), bf16),
            SHAPE((CL * NS, 2 * TOK), f32),
            SHAPE((CL * NS, 2 * TOK), f32),
        ],
        scratch_shapes=[pltpu.VMEM((NS * CC, TOK), f32)],
        name="conv",
    )(cols, skip, *tabs)


def back(gg, cols, mixed, sig, tap, skip, tabs):
    return pl.pallas_call(
        back_kernel,
        grid=(STEPS,),
        in_specs=[WIDE, PACK, PLAIN, SPEC, SPEC, LANE] + [whole(t) for t in tabs],
        out_specs=[PACK, LANE],
        out_shape=[SHAPE((NS, 3, CL, TOK), bf16), SHAPE((CL, TOK), f32)],
        scratch_shapes=[pltpu.VMEM((NS * CC, TOK), f32)] * 2,
        name="back",
    )(gg, cols, mixed, sig, tap, skip, *tabs)


def to_cols_kernel(s_ref, f_ref, g_ref, out_ref):
    for i, ref in enumerate((s_ref, f_ref, g_ref)):
        for b in range(ref.shape[1] // TOK):
            turned = ref[:, b * TOK : (b + 1) * TOK].T
            for j in range(TOK // CL):
                out_ref[b * (TOK // CL) + j, i] = turned[j * CL : (j + 1) * CL, :]


def to_cols(signal, taps, gate):
    width = signal.shape[1]
    span = 4 * TOK
    block = pl.BlockSpec((TOK, span), lambda i: (0, i))
    return pl.pallas_call(
        to_cols_kernel,
        grid=(width // span,),
        in_specs=[block] * 3,
        out_specs=pl.BlockSpec((span // CL, 3, CL, TOK), lambda i: (i, 0, 0, 0)),
        out_shape=SHAPE((NS, 3, CL, TOK), bf16),
        name="to_cols",
    )(signal, taps, gate)


def to_rows_kernel(in_ref, a_ref, b_ref, c_ref):
    for i, ref in enumerate((a_ref, b_ref, c_ref)):
        for b in range(ref.shape[1] // TOK):
            first = b * (TOK // CL)
            stacked = jnp.concatenate([in_ref[first + j, i] for j in range(TOK // CL)], axis=0)
            ref[:, b * TOK : (b + 1) * TOK] = stacked.T


def to_rows(cols):
    span = 4 * TOK
    block = pl.BlockSpec((TOK, span), lambda i: (0, i))
    out = SHAPE((TOK, NS * CL), bf16)
    return pl.pallas_call(
        to_rows_kernel,
        grid=(NS * CL // span,),
        in_specs=[pl.BlockSpec((span // CL, 3, CL, TOK), lambda i: (i, 0, 0, 0))],
        out_specs=[block] * 3,
        out_shape=[out] * 3,
        name="to_rows",
    )(cols)


OWN = (3, 2, 1, 6, 7, 0)
SENT = (4, 5)


def product(at, offsets, ws, cot_ref):
    y, z = at[0], at[1]
    total = None
    for r, w in enumerate(ws):
        rows = [
            w[pl.ds(pl.multiple_of((b * NZ + (z + offset) % NZ) * CL, CL), CL), :]
            for offset in offsets
            for b in range(NY)
        ]
        part = lax.dot_general(
            jnp.concatenate(rows, axis=0),
            cot_ref[(y + r) % NY],
            (((1,), (1,)), ((), ())),
            preferred_element_type=f32,
        )
        total = part if total is None else total + part
    return total


def opening_kernel(at, w0, w1, w2, w3, m0, m1, m2, m3, o0, o1, o2, o3, cot_ref, up_ref, down_ref):
    x, core = at[2], at[3]
    for s, (m, o) in enumerate(((m0, o0), (m1, o1), (m2, o2), (m3, o3))):
        mine, other = m[...], o[...]
        first = jnp.where(core == 0, mine, other)
        second = jnp.where(core == 0, other, mine)
        cot_ref[(x + s) % NX] = jnp.concatenate([first, second], axis=1)
    total = product(at, SENT, (w0, w1, w2, w3), cot_ref)
    up_ref[...] = total[: NY * CL].astype(bf16)
    down_ref[...] = total[NY * CL :].astype(bf16)


def opening_part(at, ws, mine, other):
    c, f = ws[0].shape
    t = mine[0].shape[0]
    span = 4 * TOK
    chain = pl.BlockSpec((NY * CL, span), lambda i, at: (0, i))
    return pl.pallas_call(
        opening_kernel,
        grid_spec=pltpu.PrefetchScalarGridSpec(
            num_scalar_prefetch=1,
            grid=(t // span,),
            in_specs=[pl.BlockSpec((c, f), lambda i, at: (0, 0))] * NY
            + [pl.BlockSpec((span, f // NH), lambda i, at: (i, 0))] * (2 * NX),
            out_specs=[pl.BlockSpec((NX, span, f), lambda i, at: (0, i, 0)), chain, chain],
        ),
        out_shape=[SHAPE((NX, t, f), bf16), SHAPE((NY * CL, t), bf16), SHAPE((NY * CL, t), bf16)],
        name="opening",
    )(at, *ws, *mine, *other)


def staying_kernel(at, w0, w1, w2, w3, cot_ref, own_ref):
    total = product(at, OWN, (w0, w1, w2, w3), cot_ref)
    for i in range(len(OWN)):
        own_ref[i] = total[i * NY * CL : (i + 1) * NY * CL]


def staying_part(at, ws, cot_all):
    c, f = ws[0].shape
    t = cot_all.shape[1]
    span = 4 * TOK
    return pl.pallas_call(
        staying_kernel,
        grid_spec=pltpu.PrefetchScalarGridSpec(
            num_scalar_prefetch=1,
            grid=(t // span,),
            in_specs=[pl.BlockSpec((c, f), lambda i, at: (0, 0))] * NY
            + [pl.BlockSpec((NX, span, f), lambda i, at: (0, i, 0))],
            out_specs=pl.BlockSpec((len(OWN), NY * CL, span), lambda i, at: (0, 0, i)),
        ),
        out_shape=SHAPE((len(OWN), NY * CL, t), f32),
        name="staying",
    )(at, *ws, cot_all)


def weight_kernel(at, *refs):
    pieces, cot_ref, outs, gated = refs[:NZ], refs[NZ], refs[NZ + 1 : -1], refs[-1]
    step = pl.program_id(0)

    @pl.when(step == 0)
    def _():
        row = 0
        for piece in pieces:
            gated[row : row + piece.shape[0], :] = piece[...]
            row += piece.shape[0]

    part = (dot(gated[...], cot_ref[0]) * ROOT).astype(bf16)
    for i, out in enumerate(outs):

        @pl.when(step == i)
        def _():
            out[...] = part


def grad_weight_part(at, pieces, cot_all):
    c, t, f = NS * CL, cot_all.shape[1], cot_all.shape[2]
    return pl.pallas_call(
        weight_kernel,
        grid_spec=pltpu.PrefetchScalarGridSpec(
            num_scalar_prefetch=1,
            grid=(NY,),
            in_specs=[pl.BlockSpec(p.shape, lambda i, at: (0, 0)) for p in pieces]
            + [pl.BlockSpec((1, t, f), lambda i, at: ((at[0] + i) % NY, 0, 0))],
            out_specs=[pl.BlockSpec((c, f), lambda i, at: (0, 0))] * NY,
            scratch_shapes=[pltpu.VMEM((c, t), bf16)],
        ),
        out_shape=[SHAPE((c, f), bf16)] * NY,
        name="grad_weight",
    )(at, *pieces, cot_all)


def sum_kernel(at, a_ref, b_ref, c_ref, d_ref, out_ref):
    z = at[1]
    for r in range(NZ):
        for b in range(NY):
            rows = slice((r * NY + b) * CL, (r * NY + b + 1) * CL)
            total = a_ref[rows, :].astype(f32) + b_ref[rows, :].astype(f32)
            total = total + c_ref[rows, :].astype(f32) + d_ref[rows, :].astype(f32)
            out_ref[b, (z + r) % NZ] = total


def weight_sum(at, parts):
    c, f = parts[0].shape
    return pl.pallas_call(
        sum_kernel,
        grid_spec=pltpu.PrefetchScalarGridSpec(
            num_scalar_prefetch=1,
            grid=(f // TOK,),
            in_specs=[pl.BlockSpec((c, TOK), lambda i, at: (0, i))] * NY,
            out_specs=pl.BlockSpec((NY, NZ, CL, TOK), lambda i, at: (0, 0, 0, i)),
        ),
        out_shape=SHAPE((NY, NZ, CL, f), f32),
        name="weight_sum",
    )(at, *parts).reshape(c, f)


def shift(value, axis, by):
    count = lax.axis_size(axis)
    return lax.ppermute(value, axis, [(i, (i + by) % count) for i in range(count)])


def add(received, own):
    return (received.astype(f32) + own).astype(bf16)


def after(value, *earlier):
    return lax.optimization_barrier((value,) + earlier)[0]


def ordered(signal, gate_values, filter_taps, skip_gain, w_out, cotangent):
    tabs = [jnp.asarray(t) for t in tables()]
    seq = ("y", "z")
    at = jnp.stack([lax.axis_index(a) for a in ("y", "z", "x", "core")]).astype(jnp.int32)

    pieces = cotangent.reshape(TOK, NZ // NH, NH, TOK).transpose(2, 1, 0, 3)
    pieces = lax.all_to_all(pieces, "core", split_axis=0, concat_axis=0, tiled=True)
    piece = lax.all_to_all(pieces.reshape(NZ, TOK, TOK), "z", split_axis=0, concat_axis=0, tiled=True)
    piece = piece.reshape(NZ * TOK, TOK)

    cols = to_cols(after(signal, pieces), filter_taps, gate_values)
    cols = lax.all_to_all(cols, seq, split_axis=0, concat_axis=0, tiled=True)
    ws = [w_out, shift(w_out, "y", -1), shift(w_out, "y", 2), shift(w_out, "y", 1)]
    skip = jnp.broadcast_to(skip_gain[:, None], (CL, TOK))

    other = shift(piece, "core", 1)
    mine = [piece, shift(piece, "x", -1), shift(piece, "x", 2), shift(piece, "x", 1)]
    mixed, gated, sig_spec, tap_spec = conv(cols, skip, tabs)
    gated = lax.all_to_all(gated, "y", split_axis=0, concat_axis=0, tiled=True)
    gated = gated.reshape(NY * CL, NZ * TOK)
    other = [other] + [shift(m, "core", 1) for m in mine[1:]]

    cot_all, up, down = opening_part(at, ws, mine, other)
    up = shift(up, "z", 1)
    down = shift(down, "z", -1)
    own = staying_part(at, ws, cot_all)

    for i in range(2):
        up, down = lax.optimization_barrier((up, down))
        up, down = add(up, own[i]), add(down, own[3 + i])
        up = shift(up, "z", 1)
        down = shift(down, "z", -1)
    up, down = lax.optimization_barrier((up, down))
    rest = down.astype(f32) + own[5]
    up = shift(add(up, own[2]), "z", 1)
    part = (up.astype(f32) + rest).astype(bf16)

    fore, aft = [gated], [gated]
    for _ in range(3):
        fore.append(shift(fore[-1], "z", 1))
        aft.append(shift(aft[-1], "z", -1))
    far = shift(fore[-1], "z", 1)
    ring = [gated] + aft[1:] + [far] + fore[:0:-1]

    part = part.reshape(NY, CL, NZ * TOK)
    grad_gated = lax.all_to_all(part, "y", split_axis=0, concat_axis=0, tiled=True)
    skip_again = jnp.broadcast_to(after(skip_gain, gated)[:, None], (CL, TOK))
    outs, skip_sum = back(grad_gated, cols, mixed, sig_spec, tap_spec, skip_again, tabs)
    outs_rows = lax.all_to_all(outs, seq, split_axis=0, concat_axis=0, tiled=True)
    kept, up1, up2, up3 = grad_weight_part(after(at, skip_sum), ring, cot_all)
    moved = [shift(up1, "y", 1), shift(up2, "y", 2), shift(up3, "y", -1)]
    weight = weight_sum(at, [kept] + moved)
    grad_input, grad_filter, grad_gate = to_rows(outs_rows)
    return (grad_input, grad_gate, grad_filter, jnp.sum(skip_sum, axis=1), weight)


def solution(mesh):
    fine = Mesh(mesh.devices.reshape(NY, NZ, NX, NH), ("y", "z", "x", "core"))
    seq, ch = ("y", "z"), ("x", "core")
    rows = P(seq, ch)
    vector = P(ch + seq)
    weights = P(ch, seq)
    return jax.shard_map(
        ordered,
        mesh=fine,
        in_specs=(rows, rows, rows, vector, weights, rows),
        out_specs=(rows, rows, rows, vector, weights),
        check_vma=False,
    )
```
